32 devices in a mesh: rep: 2 (over x), exp: 2 (over core), tp: 8 (over z, y).
Axes of the slice: x: 2, y: 2, z: 4, core: 2. Of those that a mesh axis runs over, the one named last changes fastest.
Arguments:
- tokens: bfloat16 [128, 4096], P(('rep', 'exp', 'tp')), parts along dimension 0, may hold values from -6 to 6
- expert_ids: int32 [128, 2], P(('rep', 'exp', 'tp')), parts along dimension 0, may hold values from 0 to 3, all different within a row; in each aligned block of 4 rows (0 to 3, 4 to 7, ...) at most 4 rows name the same one
- gate_ints: int32 [128, 2], P(('rep', 'exp', 'tp')), parts along dimension 0, may hold values from 16 to 240, as said below
- gate_weight: bfloat16 [4, 4096, 14336], P('exp', None, 'tp'), may hold values from -0.09375 to 0.09375
- up_weight: bfloat16 [4, 4096, 14336], P('exp', None, 'tp'), may hold values from -0.09375 to 0.09375
- down_weight: bfloat16 [4, 14336, 4096], P('exp', 'tp'), may hold values from -0.046875 to 0.046875
Outputs:
- mixed: bfloat16 [128, 4096], P(('rep', 'exp', 'tp')), parts along dimension 0
The draws below stay inside these ranges and needn't reach their ends.
There are 2 independent parts, one for each index of `rep`. The reference program is written for one: setup_inputs(seed, part) draws one part's arguments, and reference() takes and returns one part's arrays. A program takes and returns all parts, laid end to end along the dimension named above; an argument that names none is the same for every part. Nothing has to cross between parts.
Inputs may be any that keep to these rules, and one draw needn't show every extreme that they name: `expert_ids`: each row names two different experts. Among the 4 rows of one device an expert is named at most 4 times, and exactly that often on some device. `gate_ints`: the two entries of a row sum to 256.
All inputs are finite; a program needn't handle non-finite values.
Results may differ from the reference program's by a relative error of at most 0.0049.
Values may be sent and summed in bfloat16 or wider, within the bound.
A program may use at most 128 MiB of HBM per device.

```python
import math
import jax
import jax.numpy as jnp
import numpy as np
from jax import lax

D = 4096
FF = 14336
TOK_DEV = 4
EXPERTS = 4
TOKENS = 64


def draw_gate_ints(key, part):
    first = jax.random.randint(key, (TOKENS,), 16, 241)
    first = first.at[0].set(16)
    return jnp.stack([first, 256 - first], axis=1).astype(jnp.int32)


def block_scale(stream_key, shape, pieces, smallest, largest):
    gain = 1.0
    for axis_at, blocks in pieces:
        steps = jax.random.uniform(jax.random.fold_in(jax.random.fold_in(stream_key, 6), axis_at), (blocks,), jnp.float32, smallest / len(pieces), largest / len(pieces))
        gain = gain * jnp.repeat(jnp.exp(steps), shape[axis_at] // blocks).reshape((-1,) + (1,) * (len(shape) - 1 - axis_at))
    return gain


def assign_block(key, own, number, rows, amount, top, bound, slope):
    sequence = jax.random.permutation(key, amount)
    crowded, usual = load_shares(amount, rows * top, bound, slope, True), load_shares(amount, rows * top, bound, slope, False)
    places = jnp.arange(amount)

    def named(tallies, turn):
        used = int((tallies > 0).sum())
        fixed = max(1, used // 4)
        passed = fixed + (places - fixed + turn * (used - fixed)) % max(1, amount - fixed)
        return jnp.zeros((amount,), jnp.int32).at[sequence[jnp.where(places < fixed, places, passed)]].set(jnp.asarray(tallies, jnp.int32))

    tallies = jnp.where(number % 4 == 0, named(crowded, number // 4), named(usual, number - number // 4 - 1))
    mixed = jax.random.permutation(jax.random.fold_in(own, 3), amount)
    giver, sink = mixed[0:amount // 2 * 2:2], mixed[1:amount // 2 * 2:2]
    slack = jnp.minimum(tallies[giver] - 1, bound - tallies[sink]) // 2
    slack = jnp.where((giver == sequence[0]) | (sink == sequence[0]) | (tallies[sink] == 0), 0, jnp.maximum(slack, 0))
    passed = jax.random.randint(jax.random.fold_in(own, 4), (amount // 2,), 0, 1 << 20) % (slack + 1)
    tallies = tallies.at[giver].add(-passed).at[sink].add(passed)
    items = jnp.searchsorted(jnp.cumsum(tallies), jnp.arange(rows * top), side="right").astype(jnp.int32)
    table = items.reshape(top, rows).T
    table = table[jax.random.permutation(jax.random.fold_in(own, 1), rows)]
    turn = jax.random.randint(jax.random.fold_in(own, 2), (rows, 1), 0, top)
    return jnp.take_along_axis(table, (jnp.arange(top)[None, :] + turn) % top, axis=1)


def load_shares(amount, total, bound, lean, full):
    loads = [(1 << 20) // math.isqrt(grade ** lean) + 1 for grade in range(1, amount + 1)]
    largest = bound if full else min(bound, max(-(-total // amount), total * loads[0] // sum(loads)))
    least = 1 if total - largest >= amount - 1 else 0
    given, spare = [largest] + [least] * (amount - 1), total - largest - least * (amount - 1)
    while spare > 0:
        candidates = [i for i in range(1, amount) if given[i] < largest] or [i for i in range(1, amount) if given[i] < bound]
        whole, left = sum([loads[i] for i in candidates]), spare
        for i in candidates:
            more = min(bound - given[i], max(1, left * loads[i] // whole), spare)
            given[i] = given[i] + more
            spare = spare - more
    return np.array(given)


def gaussian(key, extent, width, bound, pieces=(), kind=jnp.bfloat16):
    loudness = block_scale(key, extent, pieces, -0.22, 0.18) if pieces else 1.0
    drawn = jax.random.normal(key, extent, jnp.float32) * width * loudness
    return jnp.minimum(jnp.maximum(drawn, -bound), bound).astype(kind)


def setup_inputs(seed: int = 0, part: int = 0) -> dict:
    seeds = jax.random.split(jax.random.key(seed), 7)
    part_keys = jax.random.split(jax.random.fold_in(seeds[6], part), 7)
    tokens = gaussian(part_keys[0], (TOKENS, D), 1.0, 6.0, ((0, 16),))
    expert_ids_keys = jax.random.split(jax.random.fold_in(part_keys[1], 1), TOKENS // TOK_DEV)
    expert_ids_turns = jax.random.permutation(jax.random.fold_in(part_keys[1], 3), TOKENS // TOK_DEV)
    expert_ids = jax.vmap(lambda own, number: assign_block(jax.random.fold_in(part_keys[1], 2), own, number, TOK_DEV, EXPERTS, 2, TOK_DEV, 1))(expert_ids_keys, expert_ids_turns).reshape((TOKENS, 2))
    gate_ints = draw_gate_ints(jax.random.fold_in(jax.random.fold_in(seeds[6], part), 71), part)
    gate_weight = gaussian(seeds[3], (EXPERTS, D, FF), D ** -0.5, 0.09375, ((0, 2), (2, 8)))
    up_weight = gaussian(seeds[4], (EXPERTS, D, FF), D ** -0.5, 0.09375, ((0, 2), (2, 8)))
    down_weight = gaussian(seeds[5], (EXPERTS, FF, D), FF ** -0.5, 0.046875, ((0, 2), (1, 8)))
    return dict(tokens=tokens, expert_ids=expert_ids, gate_ints=gate_ints, gate_weight=gate_weight, up_weight=up_weight, down_weight=down_weight)


def reference(tokens, expert_ids, gate_ints, gate_weight, up_weight, down_weight):
    inputs = tokens.astype(jnp.float32)
    gates = gate_ints.astype(jnp.float32) / 256.0

    def accumulate(index, total):
        w_gate = gate_weight[index].astype(jnp.float32)
        w_up = up_weight[index].astype(jnp.float32)
        w_down = down_weight[index].astype(jnp.float32)
        gate = jnp.dot(inputs, w_gate, preferred_element_type=jnp.float32)
        upper = jnp.dot(inputs, w_up, preferred_element_type=jnp.float32)
        hidden = (jax.nn.silu(gate) * upper).astype(jnp.bfloat16)
        output = jnp.dot(hidden.astype(jnp.float32), w_down, preferred_element_type=jnp.float32)
        weight = jnp.sum(jnp.where(expert_ids == index, gates, 0.0), axis=1)
        return total + weight[:, None] * output

    start = jnp.zeros((TOKENS, D), jnp.float32)
    total = lax.fori_loop(0, EXPERTS, accumulate, start)
    return total.astype(jnp.bfloat16)
```

```python
import functools

import jax
import jax.numpy as jnp
from jax import lax
from jax.experimental import pallas as pl
from jax.experimental.pallas import tpu as pltpu
from jax.sharding import PartitionSpec as P

MESH = pl.DeviceIdType.MESH
LANES = 128
VMEM_BYTES = 67043328


def kernel(
    dims, kc, cw, window,
    ids_ref, gates_ref, tok_ref, gw_ref, uw_ref, dw_ref, out_ref,
    xg, stage, x, wst, acc, h, wbuf, dbuf, keep, mine,
    ex_send, ex_recv, rp_send, rp_recv, tp_send, tp_recv,
    gu_sem, dn_sem, zs, rs, ys, es, g_recv,
    ex_ssem, ex_rsem, rp_ssem, rp_rsem, tp_ssem, tp_rsem,
):
    nr, nz, ny, own = dims
    nt = nz * ny
    r = lax.axis_index("rep")
    e = lax.axis_index("exp")
    t = lax.axis_index("tp")
    z, y = t // ny, t % ny
    other = 1 - e
    rows, width = tok_ref.shape
    hidden = gw_ref.shape[2]
    experts = gw_ref.shape[0]
    nk, tokens, _ = x.shape
    half = tokens // 2
    quarter = nt * rows
    nc = width // cw
    group = stage.shape[0] // rows

    def slot_of(ee, rr, tt):
        return (ee * nr + rr) * nt + tt

    me = slot_of(e, r, t)

    def gu_copies(l, k):
        return [
            pltpu.make_async_copy(
                ref.at[r * own + l, pl.ds(k * kc, kc), :],
                wbuf.at[l, m, pl.ds(k * kc, kc), :],
                gu_sem.at[l, m, k],
            )
            for m, ref in enumerate((gw_ref, uw_ref))
        ]

    def dn_copies(c):
        return [
            pltpu.make_async_copy(
                dw_ref.at[r * own + l, :, pl.ds(c * cw, cw)], dbuf.at[l, c], dn_sem.at[l, c]
            )
            for l in range(own)
        ]

    items = [functools.partial(gu_copies, l, k) for l in range(own) for k in range(nk)]
    items += [functools.partial(dn_copies, c) for c in range(nc)]
    waited = [0]

    def start(i):
        if i < len(items):
            for copy in items[i]():
                copy.start()

    def pump(upto):
        while waited[0] < upto:
            for copy in items[waited[0]]():
                copy.wait()
            start(waited[0] + window)
            waited[0] += 1

    for i in range(window):
        start(i)

    barrier = pltpu.get_barrier_semaphore()

    def greet(d, carry):
        pl.semaphore_signal(
            barrier, inc=1, device_id={"tp": (t + d) % nt}, device_id_type=MESH
        )
        return carry

    lax.fori_loop(1, nt, greet, 0)
    for d in range(1, nr):
        pl.semaphore_signal(
            barrier, inc=1, device_id={"rep": (r + d) % nr}, device_id_type=MESH
        )
    pl.semaphore_signal(barrier, inc=1, device_id={"exp": other}, device_id_type=MESH)

    lane = lax.broadcasted_iota(jnp.int32, (rows, LANES), 1)
    sub = lax.broadcasted_iota(jnp.int32, (rows, LANES), 0)
    weight = jnp.zeros((rows, LANES), jnp.float32)
    for i in range(rows):
        for k in range(ids_ref.shape[0]):
            value = gates_ref[k, i].astype(jnp.float32) * (1.0 / 256.0)
            weight += jnp.where((sub == i) & (lane == ids_ref[k, i]), value, 0.0)
    xg[me, :, :width] = tok_ref[...]
    xg[me, :, width:] = weight.astype(jnp.bfloat16)

    pl.semaphore_wait(barrier, nt + nr - 1)

    def send(slot, send_sem, device):
        return pltpu.make_async_remote_copy(
            src_ref=xg.at[slot], dst_ref=xg.at[slot],
            send_sem=send_sem, recv_sem=g_recv.at[slot],
            device_id=device, device_id_type=MESH,
        )

    def z_copy(d):
        return send(me, zs.at[d], {"tp": ((z + d) % nz) * ny + y})

    def r_copy(slot, i, d):
        return send(slot, rs.at[d, i], {"rep": (r + d) % nr})

    def y_copy(slot, i, d):
        return send(slot, ys.at[d, i], {"tp": z * ny + (y + d) % ny})

    def e_copy(slot):
        return send(slot, es.at[slot % (nr * nt)], {"exp": other})

    def arrived(slot):
        send(slot, zs.at[0], {"exp": other}).wait_recv()

    def pass_y(slot, i):
        def go(d, carry):
            y_copy(slot, i, d).start()
            return carry

        lax.fori_loop(1, ny, go, 0)

    def pass_r(slot, i):
        for d in range(1, nr):
            r_copy(slot, i, d).start()

    def z_start(d, carry):
        z_copy(d).start()
        return carry

    lax.fori_loop(1, nz, z_start, 0)
    pass_r(me, z)
    pass_y(me, r * nz + z)
    e_copy(me).start()

    def z_relay(d, carry):
        zz = (z + nz - d) % nz
        slot = slot_of(e, r, zz * ny + y)
        arrived(slot)
        pass_r(slot, zz)
        pass_y(slot, r * nz + zz)
        e_copy(slot).start()
        return carry

    lax.fori_loop(1, nz, z_relay, 0)
    pump(1)

    def r_relay(i, carry):
        rr = (r + nr - 1 - i // nz) % nr
        zz = (z + nz - i % nz) % nz
        slot = slot_of(e, rr, zz * ny + y)
        arrived(slot)
        pass_y(slot, rr * nz + zz)
        e_copy(slot).start()
        return carry

    lax.fori_loop(0, (nr - 1) * nz, r_relay, 0)
    pump(2)

    def y_relay(i, carry):
        yy = (y + ny - 1 - i // (nr * nz)) % ny
        rr = (r + i // nz) % nr
        zz = (z + nz - i % nz) % nz
        slot = slot_of(e, rr, zz * ny + yy)
        arrived(slot)
        e_copy(slot).start()
        return carry

    lax.fori_loop(0, (ny - 1) * nr * nz, y_relay, 0)
    pump(4)

    def arrive(i, carry):
        arrived(other * nr * nt + i)
        return carry

    lax.fori_loop(0, nr * nt, arrive, 0)

    def lay(g, carry):
        for i in range(group):
            stage[i * rows:(i + 1) * rows, :] = xg[g * group + i].astype(jnp.float32)
        r0 = pl.multiple_of(g * group * rows, group * rows)
        for k in range(nk):
            x[k, pl.ds(r0, group * rows), :] = stage[:, k * kc:(k + 1) * kc].astype(jnp.bfloat16)
        wst[pl.ds(r0, group * rows), :] = stage[:, width:]
        return carry

    lax.fori_loop(0, tokens // (group * rows), lay, 0)

    step = 256
    for l in range(own):
        for k in range(nk):
            pump(l * nk + k + 1)
            for n in range(0, hidden, step):
                cols = slice(n, min(n + step, hidden))
                gate, upper = (
                    jnp.dot(
                        x[k], wbuf[l, m, k * kc:(k + 1) * kc, cols],
                        preferred_element_type=jnp.float32,
                    )
                    for m in range(2)
                )
                if k > 0:
                    gate = gate + acc[0, :, cols]
                    upper = upper + acc[1, :, cols]
                if k < nk - 1:
                    acc[0, :, cols] = gate
                    acc[1, :, cols] = upper
                else:
                    h[l, :, cols] = (gate / (1.0 + jnp.exp(-gate)) * upper).astype(jnp.bfloat16)

    lanes = lax.broadcasted_iota(jnp.int32, (tokens, LANES), 1)
    first = e * experts + r * own
    scales = [
        jnp.sum(jnp.where(lanes == first + l, wst[...], 0.0), axis=1, keepdims=True)
        for l in range(own)
    ]

    def ex_copy(c):
        return pltpu.make_async_remote_copy(
            src_ref=ex_send.at[c], dst_ref=ex_recv.at[c],
            send_sem=ex_ssem.at[c], recv_sem=ex_rsem.at[c],
            device_id={"exp": other}, device_id_type=MESH,
        )

    def rp_copy(c, d):
        target = (r + d) % nr
        return pltpu.make_async_remote_copy(
            src_ref=rp_send.at[c, target], dst_ref=rp_recv.at[c, d],
            send_sem=rp_ssem.at[c, d], recv_sem=rp_rsem.at[c, d],
            device_id={"rep": target}, device_id_type=MESH,
        )

    def tp_copy(c, d):
        target = (t + d) % nt
        return pltpu.make_async_remote_copy(
            src_ref=tp_send.at[c, target], dst_ref=tp_recv.at[c, t],
            send_sem=tp_ssem.at[c, d], recv_sem=tp_rsem.at[c, t],
            device_id={"tp": target}, device_id_type=MESH,
        )

    def tp_from(c, source):
        return pltpu.make_async_remote_copy(
            src_ref=tp_send.at[c, source], dst_ref=tp_recv.at[c, source],
            send_sem=tp_ssem.at[c, 0], recv_sem=tp_rsem.at[c, source],
            device_id={"tp": source}, device_id_type=MESH,
        )

    def down(c):
        pump(own * nk + c + 1)
        for n in range(0, cw, step):
            cols = slice(n, min(n + step, cw))
            total = None
            for l in range(own):
                part = scales[l] * jnp.dot(
                    h[l], dbuf[l, c, :, cols], preferred_element_type=jnp.float32
                )
                total = part if total is None else total + part
            low, high = total[:half], total[half:]
            keep[c, :, cols] = jnp.where(e == 0, low, high)
            ex_send[c, :, cols] = jnp.where(e == 0, high, low).astype(jnp.bfloat16)
        ex_copy(c).start()

    def pass_ex(c):
        ex_copy(c).wait_recv()
        picked = None
        for rr in range(nr):
            span = slice(rr * quarter, (rr + 1) * quarter)
            total = keep[c, span, :] + ex_recv[c, span, :].astype(jnp.float32)
            rp_send[c, rr] = total.astype(jnp.bfloat16)
            picked = total if picked is None else jnp.where(r == rr, total, picked)
        mine[c] = picked
        for d in range(1, nr):
            rp_copy(c, d).start()

    def pass_rp(c):
        total = mine[c]
        for d in range(1, nr):
            rp_copy(c, d).wait_recv()
            total = total + rp_recv[c, d].astype(jnp.float32)
        for j in range(nt):
            tp_send[c, j] = total[j * rows:(j + 1) * rows, :].astype(jnp.bfloat16)
        tp_recv[c, t] = tp_send[c, t]

        def go(d, carry):
            tp_copy(c, d).start()
            return carry

        lax.fori_loop(1, nt, go, 0)

    def collect(c):
        def wait(d, carry):
            tp_from(c, (t + nt - d) % nt).wait_recv()
            return carry

        lax.fori_loop(1, nt, wait, 0)
        total = tp_recv[c, 0].astype(jnp.float32)
        for j in range(1, nt):
            total += tp_recv[c, j].astype(jnp.float32)
        out_ref[:, c * cw:(c + 1) * cw] = total.astype(out_ref.dtype)

    lag_ex, lag_rp = 2, 5
    for c in range(nc):
        down(c)
        if c >= lag_ex:
            pass_ex(c - lag_ex)
        if c >= lag_rp:
            pass_rp(c - lag_rp)
    done_ex, done_rp = max(nc - lag_ex, 0), max(nc - lag_rp, 0)
    while done_rp < nc:
        if done_ex < nc:
            pass_ex(done_ex)
            done_ex += 1
        pass_rp(done_rp)
        done_rp += 1
    for c in range(nc):
        collect(c)

    def z_drain(d, carry):
        z_copy(d).wait_send()
        return carry

    lax.fori_loop(1, nz, z_drain, 0)

    def r_drain(i, carry):
        for d in range(1, nr):
            r_copy(me, i, d).wait_send()
        return carry

    lax.fori_loop(0, nz, r_drain, 0)

    def y_drain(i, carry):
        def inner(d, c):
            y_copy(me, i, d).wait_send()
            return c

        return lax.fori_loop(1, ny, inner, carry)

    lax.fori_loop(0, nr * nz, y_drain, 0)

    def e_drain(i, carry):
        e_copy(e * nr * nt + i).wait_send()
        return carry

    lax.fori_loop(0, nr * nt, e_drain, 0)

    def c_drain(c, carry):
        ex_copy(c).wait_send()
        for d in range(1, nr):
            rp_copy(c, d).wait_send()

        def inner(d, i):
            tp_copy(c, d).wait_send()
            return i

        return lax.fori_loop(1, nt, inner, carry)

    lax.fori_loop(0, nc, c_drain, 0)


def body(tokens, expert_ids, gate_ints, gate_weight, up_weight, down_weight):
    rows, width = tokens.shape
    experts, _, hidden = gate_weight.shape
    nt = lax.axis_size("tp")
    nr = lax.axis_size("rep")
    ny = 1
    while nt % (ny * 2) == 0 and (ny * 2) ** 2 <= nt:
        ny *= 2
    nz = nt // ny
    assert experts % nr == 0 and lax.axis_size("exp") == 2
    own = experts // nr
    slots = nt * nr * 2
    total = slots * rows
    kc = min(512, width)
    cw = min(512, width)
    nk, nc = width // kc, width // cw
    bf16, f32 = jnp.bfloat16, jnp.float32
    vmem = pl.BlockSpec(memory_space=pltpu.VMEM)
    smem = pl.BlockSpec(memory_space=pltpu.SMEM)
    hbm = pl.BlockSpec(memory_space=pl.ANY)
    dma = pltpu.SemaphoreType.DMA
    return pl.pallas_call(
        functools.partial(kernel, (nr, nz, ny, own), kc, cw, 4),
        out_shape=jax.ShapeDtypeStruct((rows, width), bf16),
        in_specs=[smem, smem, vmem, hbm, hbm, hbm],
        out_specs=vmem,
        scratch_shapes=[
            pltpu.VMEM((slots, rows, width + LANES), bf16),
            pltpu.VMEM((16, width + LANES), f32),
            pltpu.VMEM((nk, total, kc), bf16),
            pltpu.VMEM((total, LANES), f32),
            pltpu.VMEM((2, total, hidden), f32),
            pltpu.VMEM((own, total, hidden), bf16),
            pltpu.VMEM((own, 2, width, hidden), bf16),
            pltpu.VMEM((own, nc, hidden, cw), bf16),
            pltpu.VMEM((nc, total // 2, cw), f32),
            pltpu.VMEM((nc, nt * rows, cw), f32),
            pltpu.VMEM((nc, total // 2, cw), bf16),
            pltpu.VMEM((nc, total // 2, cw), bf16),
            pltpu.VMEM((nc, nr, nt * rows, cw), bf16),
            pltpu.VMEM((nc, nr, nt * rows, cw), bf16),
            pltpu.VMEM((nc, nt, rows, cw), bf16),
            pltpu.VMEM((nc, nt, rows, cw), bf16),
            dma((own, 2, nk)),
            dma((own, nc)),
            dma((nz,)),
            dma((nr, nz)),
            dma((ny, nr * nz)),
            dma((nr * nt,)),
            dma((slots,)),
            dma((nc,)),
            dma((nc,)),
            dma((nc, nr)),
            dma((nc, nr)),
            dma((nc, nt)),
            dma((nc, nt)),
        ],
        compiler_params=pltpu.CompilerParams(
            collective_id=0, has_side_effects=True, vmem_limit_bytes=VMEM_BYTES
        ),
    )(expert_ids.T, gate_ints.T, tokens, gate_weight, up_weight, down_weight)


def solution(mesh):
    return jax.shard_map(
        body,
        mesh=mesh,
        in_specs=(
            P(("rep", "exp", "tp"), None),
            P(("rep", "exp", "tp"), None),
            P(("rep", "exp", "tp"), None),
            P("exp", None, "tp"),
            P("exp", None, "tp"),
            P("exp", "tp", None),
        ),
        out_specs=P(("rep", "exp", "tp"), None),
        check_vma=False,
    )
```

```python
import functools

import jax
import jax.numpy as jnp
from jax import lax
from jax.experimental import pallas as pl
from jax.experimental.pallas import tpu as pltpu
from jax.sharding import PartitionSpec as P

MESH = pl.DeviceIdType.MESH
LANES = 128
VMEM_BYTES = 67043328
GREET_ALL = False


def kernel(
    dims, kc, cw, pieces, staged,
    ids_hbm, gates_hbm, tok_hbm, gw_ref, uw_ref, dw_ref, out_ref,
    ids_ref, gates_ref, xg, stage, x, wst, acc, h, wbuf, dbuf, keep, mine_a,
    ex_send, ex_recv, a_send, a_recv, b_send, b_recv, f_send, f_recv,
    in_sem, gu_sem, dn_sem, zs, as_, bs, es, g_recv,
    ex_ssem, ex_rsem, a_ssem, a_rsem, b_ssem, b_rsem, f_ssem, f_rsem,
):
    na, nb, nz, ny, own, swap = dims
    r = lax.axis_index("rep")
    e = lax.axis_index("exp")
    t = lax.axis_index("tp")
    z, y = t // ny, t % ny
    other = 1 - e
    turn = e if swap else 0
    a, b = r + turn * (y - r), y + turn * (r - y)
    rows, width = tok_hbm.shape
    hidden = gw_ref.shape[2]
    experts = gw_ref.shape[0]
    nk, tokens, _ = x.shape
    half = tokens // 2
    part_a, part_b = half // na, half // na // nb
    nc = width // cw
    wk = width // pieces
    group = stage.shape[0] // rows
    nab, nf = na * nb * nz, nb * nz

    def slot_of(ee, aa, bb, zz):
        return ((ee * na + aa) * nb + bb) * nz + zz

    def device(aa, bb, zz):
        return {"rep": aa + turn * (bb - aa), "tp": zz * ny + bb + turn * (aa - bb)}

    def near(i):
        m = jnp.minimum(z, nz - 1 - z)
        both = (1 - 2 * ((i + 1) % 2)) * ((i + 1) // 2)
        one = jnp.where(z < nz - 1 - z, 1, -1) * (i - m)
        return z + jnp.where(i <= 2 * m, both, one)

    me = slot_of(e, a, b, z)

    barrier = pltpu.get_barrier_semaphore()
    greeted = 0

    def greet(device_id):
        pl.semaphore_signal(barrier, inc=1, device_id=device_id, device_id_type=MESH)

    for d in range(1, nz):
        greet(device(a, b, (z + d) % nz))
        greeted += 1
    for d in range(1, na):
        greet(device((a + d) % na, b, z))
        greeted += 1
    for d in range(1, nb):
        greet(device(a, (b + d) % nb, z))
        greeted += 1
        if GREET_ALL:
            for i in range(1, nz):
                greet(device(a, (b + d) % nb, (z + i) % nz))
                greeted += 1
    greet({"exp": other})
    greeted += 1

    def load_own():
        copies = [
            pltpu.make_async_copy(
                tok_hbm.at[:, pl.ds(p * wk, wk)], xg.at[p, me, :, pl.ds(0, wk)], in_sem.at[2 + p]
            )
            for p in range(pieces)
        ]
        copies.append(pltpu.make_async_copy(ids_hbm, ids_ref, in_sem.at[0]))
        copies.append(pltpu.make_async_copy(gates_hbm, gates_ref, in_sem.at[1]))
        return copies

    for copy in load_own():
        copy.start()

    def gu_copies(l, k):
        k0 = pl.multiple_of(k * kc, kc)
        return [
            pltpu.make_async_copy(
                ref.at[r * own + l, pl.ds(k0, kc), :],
                wbuf.at[l, m, pl.ds(k0, kc), :],
                gu_sem.at[l, m, k],
            )
            for m, ref in enumerate((gw_ref, uw_ref))
        ]

    def dn_copies(c):
        return [
            pltpu.make_async_copy(
                dw_ref.at[r * own + l, :, pl.ds(c * cw, cw)], dbuf.at[l, c], dn_sem.at[l, c]
            )
            for l in range(own)
        ]

    def gu_start(k, carry):
        for l in range(own):
            for copy in gu_copies(l, k):
                copy.start()
        return carry

    lax.fori_loop(0, nk, gu_start, 0)

    def dn_start(low, high):
        for c in range(low, min(high, nc)):
            for copy in dn_copies(c):
                copy.start()

    acc[...] = jnp.zeros_like(acc)

    for copy in load_own():
        copy.wait()
    lane = lax.broadcasted_iota(jnp.int32, (rows, LANES), 1)
    same = (
        lax.broadcasted_iota(jnp.int32, (rows, rows), 0)
        == lax.broadcasted_iota(jnp.int32, (rows, rows), 1)
    )
    weight = jnp.zeros((rows, LANES), jnp.float32)
    for k in range(ids_ref.shape[0]):
        ids, gates = (
            jnp.sum(
                jnp.where(same, jnp.broadcast_to(ref[k:k + 1, :].astype(jnp.float32), (rows, rows)), 0.0),
                axis=1, keepdims=True,
            )
            for ref in (ids_ref, gates_ref)
        )
        weight += jnp.where(lane.astype(jnp.float32) == ids, gates * (1.0 / 256.0), 0.0)
    xg[pieces - 1, me, :, wk:] = weight.astype(jnp.bfloat16)

    pl.semaphore_wait(barrier, greeted)

    def send(p, slot, send_sem, device_id):
        span = pl.ds(0, wk + LANES if p == pieces - 1 else wk)
        return pltpu.make_async_remote_copy(
            src_ref=xg.at[p, slot, :, span], dst_ref=xg.at[p, slot, :, span],
            send_sem=send_sem, recv_sem=g_recv.at[p, slot],
            device_id=device_id, device_id_type=MESH,
        )

    def z_copy(p, d):
        return send(p, me, zs.at[p, d], device(a, b, (z + d) % nz))

    def a_copy(p, slot, i, d):
        return send(p, slot, as_.at[p, d, i], device((a + d) % na, b, z))

    def b_copy(p, slot, i, d):
        return send(p, slot, bs.at[p, d, i], device(a, (b + d) % nb, z))

    def e_copy(p, slot):
        return send(p, slot, es.at[p, slot % nab], {"exp": other})

    def arrived(p, slot):
        send(p, slot, zs.at[p, 0], {"exp": other}).wait_recv()

    def pass_on(p, slot, i_a, i_b):
        if i_b is not None:
            for d in range(1, nb):
                b_copy(p, slot, i_b, d).start()
        if i_a is not None:
            for d in range(1, na):
                a_copy(p, slot, i_a, d).start()
        e_copy(p, slot).start()

    for p in range(pieces):
        for d in range(1, nz):
            z_copy(p, d).start()
        pass_on(p, me, z, a * nz + z)

    def z_relay(p):
        def go(i, carry):
            zz = near(i)
            slot = slot_of(e, a, b, zz)
            arrived(p, slot)
            pass_on(p, slot, zz, a * nz + zz)
            return carry

        lax.fori_loop(1, nz, go, 0)

    def a_relay(p):
        def go(i, carry):
            aa = (a + 1 + i // nz) % na
            zz = jnp.where(i % nz == 0, z, near(i % nz))
            slot = slot_of(e, aa, b, zz)
            arrived(p, slot)
            pass_on(p, slot, None, aa * nz + zz)
            return carry

        lax.fori_loop(0, (na - 1) * nz, go, 0)

    def b_relay(p):
        def go(i, carry):
            bb = (b + 1 + i // (na * nz)) % nb
            aa = (a + i // nz) % na
            zz = jnp.where(i % nz == 0, z, near(i % nz))
            slot = slot_of(e, aa, bb, zz)
            arrived(p, slot)
            pass_on(p, slot, None, None)
            return carry

        lax.fori_loop(0, (nb - 1) * na * nz, go, 0)

    def e_arrive(p):
        def go(i, carry):
            arrived(p, other * nab + i)
            return carry

        lax.fori_loop(0, nab, go, 0)

    nkp = nk // pieces

    def lay(p, side):
        def go(g, carry):
            slot = side * nab + g * group
            for i in range(group):
                stage[i * rows:(i + 1) * rows, :] = xg[p, slot + i].astype(jnp.float32)
            r0 = pl.multiple_of(slot * rows, group * rows)
            for k in range(nkp):
                x[p * nkp + k, pl.ds(r0, group * rows), :] = (
                    stage[:, k * kc:(k + 1) * kc].astype(jnp.bfloat16)
                )
            if p == pieces - 1:
                wst[pl.ds(r0, group * rows), :] = stage[:, wk:]
            return carry

        lax.fori_loop(0, half // (group * rows), go, 0)

    for p in range(pieces):
        z_relay(p)
    for p in range(pieces):
        a_relay(p)
    dn_start(0, 3)
    for p in range(pieces):
        b_relay(p)
    dn_start(3, nc)

    step = 256

    def dots(l, k, cols):
        k0 = pl.multiple_of(k * kc, kc)
        return (
            jnp.dot(x[k], wbuf[l, m, pl.ds(k0, kc), cols], preferred_element_type=jnp.float32)
            + acc[l, m, :, cols]
            for m in range(2)
        )

    def gu_step(k, carry):
        for l in range(own):
            for copy in gu_copies(l, k):
                copy.wait()
            for n in range(0, hidden, step):
                cols = slice(n, min(n + step, hidden))
                for m, value in enumerate(dots(l, k, cols)):
                    acc[l, m, :, cols] = value
        return carry

    def gu_last(k):
        for l in range(own):
            for copy in gu_copies(l, k):
                copy.wait()
            for n in range(0, hidden, step):
                cols = slice(n, min(n + step, hidden))
                gate, upper = dots(l, k, cols)
                h[l, :, cols] = (gate / (1.0 + jnp.exp(-gate)) * upper).astype(jnp.bfloat16)

    for p in range(pieces):
        lay(p, e)
        e_arrive(p)
        lay(p, other)
        last = p == pieces - 1
        lax.fori_loop(p * nkp, (p + 1) * nkp - (1 if last else 0), gu_step, 0)
    gu_last(nk - 1)

    lanes = lax.broadcasted_iota(jnp.int32, (tokens, LANES), 1)
    first = e * experts + r * own
    scales = [
        jnp.sum(jnp.where(lanes == first + l, wst[...], 0.0), axis=1, keepdims=True)
        for l in range(own)
    ]

    def ex_copy(c):
        return pltpu.make_async_remote_copy(
            src_ref=ex_send.at[c], dst_ref=ex_recv.at[c],
            send_sem=ex_ssem.at[c], recv_sem=ex_rsem.at[c],
            device_id={"exp": other}, device_id_type=MESH,
        )

    def sa_copy(c, d):
        target = (a + d) % na
        return pltpu.make_async_remote_copy(
            src_ref=a_send.at[c, target], dst_ref=a_recv.at[c, d],
            send_sem=a_ssem.at[c, d], recv_sem=a_rsem.at[c, d],
            device_id=device(target, b, z), device_id_type=MESH,
        )

    def sb_copy(c, d):
        target = (b + d) % nb
        return pltpu.make_async_remote_copy(
            src_ref=b_send.at[c, target], dst_ref=b_recv.at[c, d],
            send_sem=b_ssem.at[c, d], recv_sem=b_rsem.at[c, d],
            device_id=device(a, target, z), device_id_type=MESH,
        )

    def f_copy(c, d):
        if staged[c]:
            mine, target = z, (z + d) % nz
            where = device(a, b, target)
        else:
            mine = b * nz + z
            target = (mine + d) % nf
            where = device(a, target // nz, target % nz)
        return pltpu.make_async_remote_copy(
            src_ref=f_send.at[c, target], dst_ref=f_recv.at[c, mine],
            send_sem=f_ssem.at[c, d], recv_sem=f_rsem.at[c, mine],
            device_id=where, device_id_type=MESH,
        )

    def f_from(c, source):
        return pltpu.make_async_remote_copy(
            src_ref=f_send.at[c, source], dst_ref=f_recv.at[c, source],
            send_sem=f_ssem.at[c, 0], recv_sem=f_rsem.at[c, source],
            device_id={"exp": other}, device_id_type=MESH,
        )

    def down(c):
        for copy in dn_copies(c):
            copy.wait()
        for n in range(0, cw, step):
            cols = slice(n, min(n + step, cw))
            total = None
            for l in range(own):
                part = scales[l] * jnp.dot(
                    h[l], dbuf[l, c, :, cols], preferred_element_type=jnp.float32
                )
                total = part if total is None else total + part
            low, high = total[:half], total[half:]
            keep[c, :, cols] = jnp.where(e == 0, low, high)
            ex_send[c, :, cols] = jnp.where(e == 0, high, low).astype(jnp.bfloat16)
        ex_copy(c).start()

    def pass_ex(c):
        ex_copy(c).wait_recv()
        picked = None
        for aa in range(na):
            span = slice(aa * part_a, (aa + 1) * part_a)
            total = keep[c, span, :] + ex_recv[c, span, :].astype(jnp.float32)
            a_send[c, aa] = total.astype(jnp.bfloat16)
            picked = total if picked is None else jnp.where(a == aa, total, picked)
        mine_a[c] = picked
        for d in range(1, na):
            sa_copy(c, d).start()

    def send_final(c, total, count, mine):
        for j in range(count):
            f_send[c, j] = total[j * rows:(j + 1) * rows, :].astype(jnp.bfloat16)
        f_recv[c, mine] = f_send[c, mine]

        def go(d, carry):
            f_copy(c, d).start()
            return carry

        lax.fori_loop(1, count, go, 0)

    def pass_a(c):
        total = mine_a[c]
        for d in range(1, na):
            sa_copy(c, d).wait_recv()
            total = total + a_recv[c, d].astype(jnp.float32)
        if not staged[c]:
            send_final(c, total, nf, b * nz + z)
            return
        picked = None
        for bb in range(nb):
            span = total[bb * part_b:(bb + 1) * part_b]
            b_send[c, bb] = span.astype(jnp.bfloat16)
            picked = span if picked is None else jnp.where(b == bb, span, picked)
        keep[c, 0:part_b, :] = picked
        for d in range(1, nb):
            sb_copy(c, d).start()

    def pass_b(c):
        if not staged[c]:
            return
        total = keep[c, 0:part_b, :]
        for d in range(1, nb):
            sb_copy(c, d).wait_recv()
            total = total + b_recv[c, d].astype(jnp.float32)
        send_final(c, total, nz, z)

    def collect(c):
        count, mine = (nz, z) if staged[c] else (nf, b * nz + z)

        def wait(d, carry):
            f_from(c, (mine + count - d) % count).wait_recv()
            return carry

        lax.fori_loop(1, count, wait, 0)
        total = f_recv[c, 0].astype(jnp.float32)
        for j in range(1, count):
            total += f_recv[c, j].astype(jnp.float32)
        out_ref[:, c * cw:(c + 1) * cw] = total.astype(out_ref.dtype)

    def gather_drain():
        for p in range(pieces):
            for d in range(1, nz):
                z_copy(p, d).wait_send()

            def a_drain(i, carry, p=p):
                for d in range(1, na):
                    a_copy(p, me, i, d).wait_send()
                return carry

            lax.fori_loop(0, nz, a_drain, 0)

            def b_drain(i, carry, p=p):
                for d in range(1, nb):
                    b_copy(p, me, i, d).wait_send()
                return carry

            lax.fori_loop(0, na * nz, b_drain, 0)

            def e_drain(i, carry, p=p):
                e_copy(p, e * nab + i).wait_send()
                return carry

            lax.fori_loop(0, nab, e_drain, 0)

    def sum_drain(c):
        ex_copy(c).wait_send()
        for d in range(1, na):
            sa_copy(c, d).wait_send()
        if staged[c]:
            for d in range(1, nb):
                sb_copy(c, d).wait_send()

        def inner(d, carry):
            f_copy(c, d).wait_send()
            return carry

        lax.fori_loop(1, nz if staged[c] else nf, inner, 0)

    lag_ex, lag_b = 2, 3
    for c in range(nc + lag_ex):
        if c < nc:
            down(c)
        if c >= lag_ex:
            pass_ex(c - lag_ex)
    gather_drain()
    for c in range(nc + lag_b):
        if c < nc:
            pass_a(c)
        if c >= lag_b:
            pass_b(c - lag_b)
    for c in range(nc):
        sum_drain(c)
    for c in range(nc):
        collect(c)


def body(tokens, expert_ids, gate_ints, gate_weight, up_weight, down_weight):
    rows, width = tokens.shape
    experts, _, hidden = gate_weight.shape
    nt = lax.axis_size("tp")
    nr = lax.axis_size("rep")
    ny = 1
    while nt % (ny * 2) == 0 and (ny * 2) ** 2 <= nt:
        ny *= 2
    nz = nt // ny
    assert experts % nr == 0 and lax.axis_size("exp") == 2
    own = experts // nr
    slots = nt * nr * 2
    total = slots * rows
    pieces = 2
    kc = min(512, width // pieces)
    cw = min(512, width)
    nk, nc = width // kc, width // cw
    swap = nr == ny
    staged = tuple(c < nc // 2 for c in range(nc))
    bf16, f32, i32 = jnp.bfloat16, jnp.float32, jnp.int32
    vmem = pl.BlockSpec(memory_space=pltpu.VMEM)
    hbm = pl.BlockSpec(memory_space=pl.ANY)
    dma = pltpu.SemaphoreType.DMA
    part_a = total // 2 // nr
    part_b = part_a // ny
    top = expert_ids.shape[1]
    return pl.pallas_call(
        functools.partial(kernel, (nr, ny, nz, ny, own, swap), kc, cw, pieces, staged),
        out_shape=jax.ShapeDtypeStruct((rows, width), bf16),
        in_specs=[hbm] * 6,
        out_specs=vmem,
        scratch_shapes=[
            pltpu.VMEM((top, rows), i32),
            pltpu.VMEM((top, rows), i32),
            pltpu.VMEM((pieces, slots, rows, width // pieces + LANES), bf16),
            pltpu.VMEM((16, width // pieces + LANES), f32),
            pltpu.VMEM((nk, total, kc), bf16),
            pltpu.VMEM((total, LANES), f32),
            pltpu.VMEM((own, 2, total, hidden), f32),
            pltpu.VMEM((own, total, hidden), bf16),
            pltpu.VMEM((own, 2, width, hidden), bf16),
            pltpu.VMEM((own, nc, hidden, cw), bf16),
            pltpu.VMEM((nc, total // 2, cw), f32),
            pltpu.VMEM((nc, part_a, cw), f32),
            pltpu.VMEM((nc, total // 2, cw), bf16),
            pltpu.VMEM((nc, total // 2, cw), bf16),
            pltpu.VMEM((nc, nr, part_a, cw), bf16),
            pltpu.VMEM((nc, nr, part_a, cw), bf16),
            pltpu.VMEM((nc, ny, part_b, cw), bf16),
            pltpu.VMEM((nc, ny, part_b, cw), bf16),
            pltpu.VMEM((nc, nt, rows, cw), bf16),
            pltpu.VMEM((nc, nt, rows, cw), bf16),
            dma((2 + pieces,)),
            dma((own, 2, nk)),
            dma((own, nc)),
            dma((pieces, nz)),
            dma((pieces, nr, nz)),
            dma((pieces, ny, nr * nz)),
            dma((pieces, nr * nt)),
            dma((pieces, slots)),
            dma((nc,)),
            dma((nc,)),
            dma((nc, nr)),
            dma((nc, nr)),
            dma((nc, ny)),
            dma((nc, ny)),
            dma((nc, nt)),
            dma((nc, nt)),
        ],
        compiler_params=pltpu.CompilerParams(
            collective_id=0, has_side_effects=True, vmem_limit_bytes=VMEM_BYTES
        ),
    )(expert_ids.T, gate_ints.T, tokens, gate_weight, up_weight, down_weight)


def solution(mesh):
    return jax.shard_map(
        body,
        mesh=mesh,
        in_specs=(
            P(("rep", "exp", "tp"), None),
            P(("rep", "exp", "tp"), None),
            P(("rep", "exp", "tp"), None),
            P("exp", None, "tp"),
            P("exp", None, "tp"),
            P("exp", "tp", None),
        ),
        out_specs=P(("rep", "exp", "tp"), None),
        check_vma=False,
    )
```

```python
import functools

import jax
import jax.numpy as jnp
from jax import lax
from jax.experimental import pallas as pl
from jax.experimental.pallas import tpu as pltpu
from jax.sharding import PartitionSpec as P

MESH = pl.DeviceIdType.MESH
LANES = 128
VMEM_BYTES = 67043328


def kernel(
    dims, kc, cw, pieces,
    ids_hbm, gates_hbm, tok_hbm, gw_ref, uw_ref, dw_ref, out_ref,
    ids_ref, gates_ref, xg, stage, x, wst, acc, h, wbuf, dbuf, keep, mine_q,
    ex_send, ex_recv, q_send, q_recv, f_send, f_recv,
    in_sem, gu_sem, dn_sem, zs, qs, es, g_recv,
    ex_ssem, ex_rsem, q_ssem, q_rsem, f_ssem, f_rsem,
):
    nr, ny, nz, own = dims
    nq = nr * ny
    r = lax.axis_index("rep")
    e = lax.axis_index("exp")
    t = lax.axis_index("tp")
    z, q = t // ny, r * ny + t % ny
    other = 1 - e
    rows, width = tok_hbm.shape
    hidden = gw_ref.shape[2]
    experts = gw_ref.shape[0]
    tokens = x.shape[1]
    half = tokens // 2
    part = half // nq
    nk, nc = width // kc, width // cw
    wk = width // pieces
    group = stage.shape[0] // rows
    nqz = nq * nz

    def slot_of(ee, qq, zz):
        return (ee * nq + qq) * nz + zz

    def device(qq, zz):
        return {"rep": qq // ny, "tp": zz * ny + qq % ny}

    def near(i):
        m = jnp.minimum(z, nz - 1 - z)
        both = (1 - 2 * ((i + 1) % 2)) * ((i + 1) // 2)
        one = jnp.where(z < nz - 1 - z, 1, -1) * (i - m)
        return z + jnp.where(i <= 2 * m, both, one)

    me = slot_of(e, q, z)

    barrier = pltpu.get_barrier_semaphore()
    greeted = 0

    def greet(device_id):
        pl.semaphore_signal(barrier, inc=1, device_id=device_id, device_id_type=MESH)

    for d in range(1, nz):
        greet(device(q, (z + d) % nz))
        greeted += 1
    for d in range(1, nq):
        greet(device((q + d) % nq, z))
        greeted += 1
    greet({"exp": other})
    greeted += 1

    def load_own():
        copies = [
            pltpu.make_async_copy(
                tok_hbm.at[:, pl.ds(p * wk, wk)], xg.at[p, me, :, pl.ds(0, wk)], in_sem.at[2 + p]
            )
            for p in range(pieces)
        ]
        copies.append(pltpu.make_async_copy(ids_hbm, ids_ref, in_sem.at[0]))
        copies.append(pltpu.make_async_copy(gates_hbm, gates_ref, in_sem.at[1]))
        return copies

    for copy in load_own():
        copy.start()

    def gu_copies(l, k):
        k0 = pl.multiple_of(k * kc, kc)
        return [
            pltpu.make_async_copy(
                ref.at[r * own + l, pl.ds(k0, kc), :],
                wbuf.at[l, m, pl.ds(k0, kc), :],
                gu_sem.at[l, m, k],
            )
            for m, ref in enumerate((gw_ref, uw_ref))
        ]

    def dn_copies(c):
        return [
            pltpu.make_async_copy(
                dw_ref.at[r * own + l, :, pl.ds(c * cw, cw)], dbuf.at[l, c], dn_sem.at[l, c]
            )
            for l in range(own)
        ]

    def gu_start(k, carry):
        for l in range(own):
            for copy in gu_copies(l, k):
                copy.start()
        return carry

    lax.fori_loop(0, nk, gu_start, 0)

    def dn_start(low, high):
        for c in range(low, min(high, nc)):
            for copy in dn_copies(c):
                copy.start()

    for copy in load_own():
        copy.wait()
    lane = lax.broadcasted_iota(jnp.int32, (rows, LANES), 1)
    same = (
        lax.broadcasted_iota(jnp.int32, (rows, rows), 0)
        == lax.broadcasted_iota(jnp.int32, (rows, rows), 1)
    )
    weight = jnp.zeros((rows, LANES), jnp.float32)
    for k in range(ids_ref.shape[0]):
        ids, gates = (
            jnp.sum(
                jnp.where(same, jnp.broadcast_to(ref[k:k + 1, :].astype(jnp.float32), (rows, rows)), 0.0),
                axis=1, keepdims=True,
            )
            for ref in (ids_ref, gates_ref)
        )
        weight += jnp.where(lane.astype(jnp.float32) == ids, gates * (1.0 / 256.0), 0.0)
    xg[pieces - 1, me, :, wk:] = weight.astype(jnp.bfloat16)

    pl.semaphore_wait(barrier, greeted)

    def send(p, slot, send_sem, device_id):
        span = pl.ds(0, wk + LANES if p == pieces - 1 else wk)
        return pltpu.make_async_remote_copy(
            src_ref=xg.at[p, slot, :, span], dst_ref=xg.at[p, slot, :, span],
            send_sem=send_sem, recv_sem=g_recv.at[p, slot],
            device_id=device_id, device_id_type=MESH,
        )

    def z_copy(p, d):
        return send(p, me, zs.at[p, d], device(q, (z + d) % nz))

    def q_copy(p, slot, i, d):
        return send(p, slot, qs.at[p, d, i], device((q + d) % nq, z))

    def e_copy(p, slot):
        return send(p, slot, es.at[p, slot % nqz], {"exp": other})

    def arrived(p, slot):
        send(p, slot, zs.at[p, 0], {"exp": other}).wait_recv()

    def pass_q(p, slot, i):
        for d in range(1, nq):
            q_copy(p, slot, i, d).start()
        e_copy(p, slot).start()

    for p in range(pieces):
        for d in range(1, nz):
            z_copy(p, d).start()
        pass_q(p, me, z)

    def z_relay(p):
        def go(i, carry):
            zz = near(i)
            slot = slot_of(e, q, zz)
            arrived(p, slot)
            pass_q(p, slot, zz)
            return carry

        lax.fori_loop(1, nz, go, 0)

    def q_relay(p):
        def go(i, carry):
            zz = jnp.where(i // (nq - 1) == 0, z, near(i // (nq - 1)))
            slot = slot_of(e, (q + 1 + i % (nq - 1)) % nq, zz)
            arrived(p, slot)
            e_copy(p, slot).start()
            return carry

        lax.fori_loop(0, (nq - 1) * nz, go, 0)

    def e_arrive(p):
        def go(i, carry):
            arrived(p, other * nqz + i)
            return carry

        lax.fori_loop(0, nqz, go, 0)

    def lay(p, side):
        def go(g, carry):
            slot = side * nqz + g * group
            for i in range(group):
                stage[i * rows:(i + 1) * rows, :] = xg[p, slot + i].astype(jnp.float32)
            r0 = pl.multiple_of(slot * rows, group * rows)
            x[p, pl.ds(r0, group * rows), :] = stage[:, :wk].astype(jnp.bfloat16)
            if p == pieces - 1:
                wst[pl.ds(r0, group * rows), :] = stage[:, wk:]
            return carry

        lax.fori_loop(0, half // (group * rows), go, 0)

    step = 256

    def project(p):
        for l in range(own):
            for k in range(p * nk // pieces, (p + 1) * nk // pieces):
                for copy in gu_copies(l, k):
                    copy.wait()
            for n in range(0, hidden, step):
                cols = slice(n, min(n + step, hidden))
                gate, upper = (
                    jnp.dot(
                        x[p], wbuf[l, m, p * wk:(p + 1) * wk, cols],
                        preferred_element_type=jnp.float32,
                    )
                    for m in range(2)
                )
                if p > 0:
                    gate = gate + acc[l, 0, :, cols]
                    upper = upper + acc[l, 1, :, cols]
                if p < pieces - 1:
                    acc[l, 0, :, cols] = gate
                    acc[l, 1, :, cols] = upper
                else:
                    h[l, :, cols] = (gate / (1.0 + jnp.exp(-gate)) * upper).astype(jnp.bfloat16)

    for p in range(pieces):
        z_relay(p)
    dn_start(0, 3)
    for p in range(pieces):
        q_relay(p)
        if p == 0:
            dn_start(3, nc)
            lay(p, e)
    for p in range(pieces):
        if p > 0:
            lay(p, e)
        e_arrive(p)
        lay(p, other)
        project(p)

    lanes = lax.broadcasted_iota(jnp.int32, (tokens, LANES), 1)
    first = e * experts + r * own
    scales = [
        jnp.sum(jnp.where(lanes == first + l, wst[...], 0.0), axis=1, keepdims=True)
        for l in range(own)
    ]

    def ex_copy(c):
        return pltpu.make_async_remote_copy(
            src_ref=ex_send.at[c], dst_ref=ex_recv.at[c],
            send_sem=ex_ssem.at[c], recv_sem=ex_rsem.at[c],
            device_id={"exp": other}, device_id_type=MESH,
        )

    def sq_copy(c, d):
        target = (q + d) % nq
        return pltpu.make_async_remote_copy(
            src_ref=q_send.at[c, target], dst_ref=q_recv.at[c, d],
            send_sem=q_ssem.at[c, d], recv_sem=q_rsem.at[c, d],
            device_id=device(target, z), device_id_type=MESH,
        )

    def f_copy(c, d):
        target = (z + d) % nz
        return pltpu.make_async_remote_copy(
            src_ref=f_send.at[c, target], dst_ref=f_recv.at[c, d],
            send_sem=f_ssem.at[c, d], recv_sem=f_rsem.at[c, d],
            device_id=device(q, target), device_id_type=MESH,
        )

    def down(c):
        for copy in dn_copies(c):
            copy.wait()
        for n in range(0, cw, step):
            cols = slice(n, min(n + step, cw))
            total = None
            for l in range(own):
                value = scales[l] * jnp.dot(
                    h[l], dbuf[l, c, :, cols], preferred_element_type=jnp.float32
                )
                total = value if total is None else total + value
            low, high = total[:half], total[half:]
            keep[c, :, cols] = jnp.where(e == 0, low, high)
            ex_send[c, :, cols] = jnp.where(e == 0, high, low).astype(jnp.bfloat16)
        ex_copy(c).start()

    def pass_ex(c):
        ex_copy(c).wait_recv()
        picked = None
        for qq in range(nq):
            span = slice(qq * part, (qq + 1) * part)
            total = keep[c, span, :] + ex_recv[c, span, :].astype(jnp.float32)
            q_send[c, qq] = total.astype(jnp.bfloat16)
            picked = total if picked is None else jnp.where(q == qq, total, picked)
        mine_q[c] = picked
        for d in range(1, nq):
            sq_copy(c, d).start()

    def pass_q_sum(c):
        total = mine_q[c]
        for d in range(1, nq):
            sq_copy(c, d).wait_recv()
            total = total + q_recv[c, d].astype(jnp.float32)
        for j in range(nz):
            f_send[c, j] = total[j * rows:(j + 1) * rows, :].astype(jnp.bfloat16)
        f_recv[c, 0] = f_send[c, z]
        for d in range(1, nz):
            f_copy(c, d).start()

    def collect(c):
        for d in range(1, nz):
            f_copy(c, d).wait_recv()
        total = f_recv[c, 0].astype(jnp.float32)
        for d in range(1, nz):
            total += f_recv[c, d].astype(jnp.float32)
        out_ref[:, c * cw:(c + 1) * cw] = total.astype(out_ref.dtype)

    def gather_drain():
        for p in range(pieces):
            for d in range(1, nz):
                z_copy(p, d).wait_send()

            def q_drain(i, carry, p=p):
                for d in range(1, nq):
                    q_copy(p, me, i, d).wait_send()
                return carry

            lax.fori_loop(0, nz, q_drain, 0)

            def e_drain(i, carry, p=p):
                e_copy(p, e * nqz + i).wait_send()
                return carry

            lax.fori_loop(0, nqz, e_drain, 0)

    def sum_drain(c):
        ex_copy(c).wait_send()
        for d in range(1, nq):
            sq_copy(c, d).wait_send()
        for d in range(1, nz):
            f_copy(c, d).wait_send()

    lag_ex, lag_q = 2, 6
    for c in range(nc + lag_q):
        if c < nc:
            down(c)
        if lag_ex <= c < nc + lag_ex:
            pass_ex(c - lag_ex)
        if c == nc:
            gather_drain()
        if c >= lag_q:
            pass_q_sum(c - lag_q)
    for c in range(nc):
        collect(c)
    for c in range(nc):
        sum_drain(c)


def body(tokens, expert_ids, gate_ints, gate_weight, up_weight, down_weight):
    rows, width = tokens.shape
    experts, _, hidden = gate_weight.shape
    nt = lax.axis_size("tp")
    nr = lax.axis_size("rep")
    ny = 1
    while nt % (ny * 2) == 0 and (ny * 2) ** 2 <= nt:
        ny *= 2
    nz = nt // ny
    assert experts % nr == 0 and lax.axis_size("exp") == 2
    own = experts // nr
    slots = nt * nr * 2
    total = slots * rows
    pieces = 2
    kc = min(512, width // pieces)
    cw = min(512, width)
    nk, nc = width // kc, width // cw
    bf16, f32, i32 = jnp.bfloat16, jnp.float32, jnp.int32
    vmem = pl.BlockSpec(memory_space=pltpu.VMEM)
    hbm = pl.BlockSpec(memory_space=pl.ANY)
    dma = pltpu.SemaphoreType.DMA
    nq = nr * ny
    part = total // 2 // nq
    top = expert_ids.shape[1]
    return pl.pallas_call(
        functools.partial(kernel, (nr, ny, nz, own), kc, cw, pieces),
        out_shape=jax.ShapeDtypeStruct((rows, width), bf16),
        in_specs=[hbm] * 6,
        out_specs=vmem,
        scratch_shapes=[
            pltpu.VMEM((top, rows), i32),
            pltpu.VMEM((top, rows), i32),
            pltpu.VMEM((pieces, slots, rows, width // pieces + LANES), bf16),
            pltpu.VMEM((16, width // pieces + LANES), f32),
            pltpu.VMEM((pieces, total, width // pieces), bf16),
            pltpu.VMEM((total, LANES), f32),
            pltpu.VMEM((own, 2, total, hidden), f32),
            pltpu.VMEM((own, total, hidden), bf16),
            pltpu.VMEM((own, 2, width, hidden), bf16),
            pltpu.VMEM((own, nc, hidden, cw), bf16),
            pltpu.VMEM((nc, total // 2, cw), f32),
            pltpu.VMEM((nc, part, cw), f32),
            pltpu.VMEM((nc, total // 2, cw), bf16),
            pltpu.VMEM((nc, total // 2, cw), bf16),
            pltpu.VMEM((nc, nq, part, cw), bf16),
            pltpu.VMEM((nc, nq, part, cw), bf16),
            pltpu.VMEM((nc, nz, rows, cw), bf16),
            pltpu.VMEM((nc, nz, rows, cw), bf16),
            dma((2 + pieces,)),
            dma((own, 2, nk)),
            dma((own, nc)),
            dma((pieces, nz)),
            dma((pieces, nq, nz)),
            dma((pieces, nq * nz)),
            dma((pieces, slots)),
            dma((nc,)),
            dma((nc,)),
            dma((nc, nq)),
            dma((nc, nq)),
            dma((nc, nz)),
            dma((nc, nz)),
        ],
        compiler_params=pltpu.CompilerParams(
            collective_id=0, has_side_effects=True, vmem_limit_bytes=VMEM_BYTES
        ),
    )(expert_ids.T, gate_ints.T, tokens, gate_weight, up_weight, down_weight)


def solution(mesh):
    return jax.shard_map(
        body,
        mesh=mesh,
        in_specs=(
            P(("rep", "exp", "tp"), None),
            P(("rep", "exp", "tp"), None),
            P(("rep", "exp", "tp"), None),
            P("exp", None, "tp"),
            P("exp", None, "tp"),
            P("exp", "tp", None),
        ),
        out_specs=P(("rep", "exp", "tp"), None),
        check_vma=False,
    )
```

```python
import functools

import jax
import jax.numpy as jnp
from jax import lax
from jax.experimental import pallas as pl
from jax.experimental.pallas import tpu as pltpu
from jax.sharding import PartitionSpec as P

MESH = pl.DeviceIdType.MESH
LANES = 128
VMEM_BYTES = 62000000


def kernel(
    dims, cw, pieces,
    ids_hbm, gates_hbm, tok_hbm, gw_ref, uw_ref, dw_ref, out_ref,
    ids_ref, gates_ref, xg, stage, x, wst, acc, h, wbuf, dbuf, keep, mine_q,
    ex_send, ex_recv, q_send, q_recv, f_send, f_recv,
    in_sem, gu_sem, dn_sem, g_send, z_recv, g_recv, e_recv,
    s_send, ex_rsem, q_rsem, f_rsem,
):
    nr, ny, nz, own = dims
    nq = nr * ny
    r = lax.axis_index("rep")
    e = lax.axis_index("exp")
    t = lax.axis_index("tp")
    z, q = t // ny, r * ny + t % ny
    other = 1 - e
    rows, width = tok_hbm.shape
    hidden = gw_ref.shape[2]
    experts = gw_ref.shape[0]
    tokens = x.shape[1]
    half = tokens // 2
    part = half // nq
    nc = width // cw
    wk = width // pieces
    group = stage.shape[0] // rows
    nqz = nq * nz

    def slot_of(ee, qq, zz):
        return (ee * nz + zz) * nq + qq

    def device(qq, zz):
        return {"rep": qq // ny, "tp": zz * ny + qq % ny}

    def near(i):
        m = jnp.minimum(z, nz - 1 - z)
        both = (1 - 2 * ((i + 1) % 2)) * ((i + 1) // 2)
        one = jnp.where(z < nz - 1 - z, 1, -1) * (i - m)
        return z + jnp.where(i <= 2 * m, both, one)

    me = slot_of(e, q, z)

    barrier = pltpu.get_barrier_semaphore()
    greeted = 0

    def greet(device_id):
        pl.semaphore_signal(barrier, inc=1, device_id=device_id, device_id_type=MESH)

    for d in range(1, nz):
        greet(device(q, (z + d) % nz))
        greeted += 1
    for d in range(1, nq):
        greet(device((q + d) % nq, z))
        greeted += 1
    greet({"exp": other})
    greeted += 1

    def load_own():
        copies = [
            pltpu.make_async_copy(
                tok_hbm.at[:, pl.ds(p * wk, wk)], xg.at[p, me, :, pl.ds(0, wk)], in_sem.at[2 + p]
            )
            for p in range(pieces)
        ]
        copies.append(pltpu.make_async_copy(ids_hbm, ids_ref, in_sem.at[0]))
        copies.append(pltpu.make_async_copy(gates_hbm, gates_ref, in_sem.at[1]))
        return copies

    for copy in load_own():
        copy.start()

    def gu_copies(p):
        return [
            pltpu.make_async_copy(
                ref.at[r * own + l, pl.ds(p * wk, wk), :],
                wbuf.at[l, m, pl.ds(p * wk, wk), :],
                gu_sem.at[l, m, p],
            )
            for l in range(own)
            for m, ref in enumerate((gw_ref, uw_ref))
        ]

    def dn_copies(c):
        return [
            pltpu.make_async_copy(
                dw_ref.at[r * own + l, :, pl.ds(c * cw, cw)], dbuf.at[l, c], dn_sem.at[l, c]
            )
            for l in range(own)
        ]

    def gu_start(low, high):
        for p in range(low, min(high, pieces)):
            for copy in gu_copies(p):
                copy.start()

    def dn_start(low, high):
        for c in range(low, min(high, nc)):
            for copy in dn_copies(c):
                copy.start()

    ahead = max(1, pieces - 1)
    for copy in load_own():
        copy.wait()
    gu_start(0, ahead)
    lane = lax.broadcasted_iota(jnp.int32, (rows, LANES), 1)
    same = (
        lax.broadcasted_iota(jnp.int32, (rows, rows), 0)
        == lax.broadcasted_iota(jnp.int32, (rows, rows), 1)
    )
    weight = jnp.zeros((rows, LANES), jnp.float32)
    for k in range(ids_ref.shape[0]):
        ids, gates = (
            jnp.sum(
                jnp.where(same, jnp.broadcast_to(ref[k:k + 1, :].astype(jnp.float32), (rows, rows)), 0.0),
                axis=1, keepdims=True,
            )
            for ref in (ids_ref, gates_ref)
        )
        weight += jnp.where(lane.astype(jnp.float32) == ids, gates * (1.0 / 256.0), 0.0)
    xg[pieces - 1, me, :, wk:] = weight.astype(jnp.bfloat16)

    pl.semaphore_wait(barrier, greeted)

    def send(p, slot, count, send_sem, recv_sem, device_id):
        span = pl.ds(0, wk + LANES if p == pieces - 1 else wk)
        blocks = xg.at[p, pl.ds(slot, count), :, span]
        return pltpu.make_async_remote_copy(
            src_ref=blocks, dst_ref=blocks, send_sem=send_sem, recv_sem=recv_sem,
            device_id=device_id, device_id_type=MESH,
        )

    def z_copy(p, d, count=1):
        return send(
            p, me, count, g_send.at[0, p], z_recv.at[p, z], device(q, (z + d) % nz)
        )

    def q_copy(p, zz, d):
        return send(
            p, slot_of(e, q, zz), 1, g_send.at[1, p], g_recv.at[p, zz],
            device((q + d) % nq, z),
        )

    def e_copy(p, zz):
        return send(
            p, slot_of(e, 0, zz), nq, g_send.at[2, p], e_recv.at[p], {"exp": other}
        )

    def await_z(p, zz):
        send(p, 0, 1, g_send.at[0, p], z_recv.at[p, zz], {"exp": other}).wait_recv()

    def await_q(p, zz):
        send(p, 0, nq - 1, g_send.at[1, p], g_recv.at[p, zz], {"exp": other}).wait_recv()

    def await_e(p):
        send(p, 0, nqz, g_send.at[2, p], e_recv.at[p], {"exp": other}).wait_recv()

    def gather_drain():
        for p in range(pieces):
            for i, count in enumerate((nz - 1, (nq - 1) * nz, nqz)):
                send(p, 0, count, g_send.at[i, p], e_recv.at[p], {"exp": other}).wait_send()

    def pass_q(p, zz):
        for d in range(1, nq):
            q_copy(p, zz, d).start()

    def z_start(p):
        for d in range(1, nz):
            z_copy(p, d).start()

    def z_relay(p):
        def go(i, carry):
            zz = near(i)
            await_z(p, zz)
            pass_q(p, zz)
            return carry

        lax.fori_loop(1, nz, go, 0)

    def q_relay(p, low, high):
        def go(i, carry):
            zz = jnp.where(i == 0, z, near(i))
            await_q(p, zz)
            e_copy(p, zz).start()
            return carry

        lax.fori_loop(low, high, go, 0)

    z_start(0)
    pass_q(0, z)
    for p in range(1, pieces):
        z_start(p)

    def lay(p, side):
        def go(g, carry):
            for i in range(group):
                place = g * group + i
                slot = slot_of(side, place // nz, place % nz)
                stage[i * rows:(i + 1) * rows, :] = xg[p, slot].astype(jnp.float32)
            r0 = pl.multiple_of(side * half + g * group * rows, group * rows)
            x[p, pl.ds(r0, group * rows), :] = stage[:, :wk].astype(jnp.bfloat16)
            if p == pieces - 1:
                wst[pl.ds(r0, group * rows), :] = stage[:, wk:]
            return carry

        lax.fori_loop(0, half // (group * rows), go, 0)

    step = 256

    def project(p):
        for copy in gu_copies(p):
            copy.wait()
        for l in range(own):
            for n in range(0, hidden, step):
                cols = slice(n, min(n + step, hidden))
                gate, upper = (
                    jnp.dot(
                        x[p], wbuf[l, m, p * wk:(p + 1) * wk, cols],
                        preferred_element_type=jnp.float32,
                    )
                    for m in range(2)
                )
                if p > 0:
                    gate = gate + acc[l, 0, :, cols]
                    upper = upper + acc[l, 1, :, cols]
                if p < pieces - 1:
                    acc[l, 0, :, cols] = gate
                    acc[l, 1, :, cols] = upper
                else:
                    h[l, :, cols] = (gate / (1.0 + jnp.exp(-gate)) * upper).astype(jnp.bfloat16)

    for p in range(pieces):
        z_relay(p)
        if p == 0:
            gu_start(ahead, pieces)
            dn_start(0, 2)
        if p + 1 < pieces:
            pass_q(p + 1, z)
    q_relay(0, 0, nz)
    dn_start(2, nc)
    for p in range(pieces):
        lay(p, e)
        if p + 1 < pieces:
            q_relay(p + 1, 0, nz)
        await_e(p)
        lay(p, other)
        project(p)

    lanes = lax.broadcasted_iota(jnp.int32, (tokens, LANES), 1)
    first = e * experts + r * own
    scales = [
        jnp.sum(jnp.where(lanes == first + l, wst[...], 0.0), axis=1, keepdims=True)
        for l in range(own)
    ]

    def ex_copy(c):
        return pltpu.make_async_remote_copy(
            src_ref=ex_send.at[c], dst_ref=ex_recv.at[c],
            send_sem=s_send.at[0], recv_sem=ex_rsem.at[c],
            device_id={"exp": other}, device_id_type=MESH,
        )

    def sq_copy(c, d):
        target = (q + d) % nq
        return pltpu.make_async_remote_copy(
            src_ref=q_send.at[c, target], dst_ref=q_recv.at[c, d],
            send_sem=s_send.at[1], recv_sem=q_rsem.at[c],
            device_id=device(target, z), device_id_type=MESH,
        )

    def f_copy(c, d):
        target = (z + d) % nz
        return pltpu.make_async_remote_copy(
            src_ref=f_send.at[c, target], dst_ref=f_recv.at[c, d],
            send_sem=s_send.at[2], recv_sem=f_rsem.at[c],
            device_id=device(q, target), device_id_type=MESH,
        )

    def await_sum(buffer, recv_sem, c):
        blocks = buffer.at[c, pl.ds(1, buffer.shape[1] - 1)]
        pltpu.make_async_remote_copy(
            src_ref=blocks, dst_ref=blocks, send_sem=s_send.at[0], recv_sem=recv_sem.at[c],
            device_id={"exp": other}, device_id_type=MESH,
        ).wait_recv()

    def sum_drain():
        for i, blocks in enumerate((
            ex_send, q_send.at[:, pl.ds(1, nq - 1)], f_send.at[:, pl.ds(1, nz - 1)]
        )):
            pltpu.make_async_remote_copy(
                src_ref=blocks, dst_ref=blocks, send_sem=s_send.at[i], recv_sem=ex_rsem.at[0],
                device_id={"exp": other}, device_id_type=MESH,
            ).wait_send()

    def down(c):
        for copy in dn_copies(c):
            copy.wait()
        for n in range(0, cw, step):
            cols = slice(n, min(n + step, cw))
            total = None
            for l in range(own):
                value = scales[l] * jnp.dot(
                    h[l], dbuf[l, c, :, cols], preferred_element_type=jnp.float32
                )
                total = value if total is None else total + value
            low, high = total[:half], total[half:]
            keep[c, :, cols] = jnp.where(e == 0, low, high)
            ex_send[c, :, cols] = jnp.where(e == 0, high, low).astype(jnp.bfloat16)
        ex_copy(c).start()

    def pass_ex(c):
        ex_copy(c).wait_recv()
        picked = None
        for qq in range(nq):
            span = slice(qq * part, (qq + 1) * part)
            total = keep[c, span, :] + ex_recv[c, span, :].astype(jnp.float32)
            q_send[c, qq] = total.astype(jnp.bfloat16)
            picked = total if picked is None else jnp.where(q == qq, total, picked)
        mine_q[c] = picked
        for d in range(1, nq):
            sq_copy(c, d).start()

    def pass_q_sum(c):
        total = mine_q[c]
        await_sum(q_recv, q_rsem, c)
        for d in range(1, nq):
            total = total + q_recv[c, d].astype(jnp.float32)
        for j in range(nz):
            f_send[c, j] = total[j * rows:(j + 1) * rows, :].astype(jnp.bfloat16)
        f_recv[c, 0] = f_send[c, z]
        for d in range(1, nz):
            f_copy(c, d).start()

    def collect(c):
        await_sum(f_recv, f_rsem, c)
        total = f_recv[c, 0].astype(jnp.float32)
        for d in range(1, nz):
            total += f_recv[c, d].astype(jnp.float32)
        out_ref[:, c * cw:(c + 1) * cw] = total.astype(out_ref.dtype)

    lag_ex, lag_q = 2, 6
    for c in range(nc + lag_q):
        if c < nc:
            down(c)
        if lag_ex <= c < nc + lag_ex:
            pass_ex(c - lag_ex)
        if c == nc:
            gather_drain()
        if c >= lag_q:
            pass_q_sum(c - lag_q)
    for c in range(nc):
        collect(c)
    sum_drain()


def body(tokens, expert_ids, gate_ints, gate_weight, up_weight, down_weight):
    rows, width = tokens.shape
    experts, _, hidden = gate_weight.shape
    nt = lax.axis_size("tp")
    nr = lax.axis_size("rep")
    ny = 1
    while nt % (ny * 2) == 0 and (ny * 2) ** 2 <= nt:
        ny *= 2
    nz = nt // ny
    assert experts % nr == 0 and lax.axis_size("exp") == 2
    own = experts // nr
    slots = nt * nr * 2
    total = slots * rows
    pieces = 2
    cw = min(512, width)
    nc = width // cw
    bf16, f32, i32 = jnp.bfloat16, jnp.float32, jnp.int32
    vmem = pl.BlockSpec(memory_space=pltpu.VMEM)
    hbm = pl.BlockSpec(memory_space=pl.ANY)
    dma = pltpu.SemaphoreType.DMA
    nq = nr * ny
    part = total // 2 // nq
    top = expert_ids.shape[1]
    return pl.pallas_call(
        functools.partial(kernel, (nr, ny, nz, own), cw, pieces),
        out_shape=pltpu.VMEM((rows, width), bf16),
        in_specs=[hbm] * 6,
        out_specs=vmem,
        scratch_shapes=[
            pltpu.VMEM((top, rows), i32),
            pltpu.VMEM((top, rows), i32),
            pltpu.VMEM((pieces, slots, rows, width // pieces + LANES), bf16),
            pltpu.VMEM((16, width // pieces + LANES), f32),
            pltpu.VMEM((pieces, total, width // pieces), bf16),
            pltpu.VMEM((total, LANES), f32),
            pltpu.VMEM((own, 2, total, hidden), f32),
            pltpu.VMEM((own, total, hidden), bf16),
            pltpu.VMEM((own, 2, width, hidden), bf16),
            pltpu.VMEM((own, nc, hidden, cw), bf16),
            pltpu.VMEM((nc, total // 2, cw), f32),
            pltpu.VMEM((nc, part, cw), f32),
            pltpu.VMEM((nc, total // 2, cw), bf16),
            pltpu.VMEM((nc, total // 2, cw), bf16),
            pltpu.VMEM((nc, nq, part, cw), bf16),
            pltpu.VMEM((nc, nq, part, cw), bf16),
            pltpu.VMEM((nc, nz, rows, cw), bf16),
            pltpu.VMEM((nc, nz, rows, cw), bf16),
            dma((2 + pieces,)),
            dma((own, 2, pieces)),
            dma((own, nc)),
            dma((3, pieces)),
            dma((pieces, nz)),
            dma((pieces, nz)),
            dma((pieces,)),
            dma((3,)),
            dma((nc,)),
            dma((nc,)),
            dma((nc,)),
        ],
        compiler_params=pltpu.CompilerParams(
            collective_id=0, has_side_effects=True, vmem_limit_bytes=VMEM_BYTES
        ),
    )(expert_ids.T, gate_ints.T, tokens, gate_weight, up_weight, down_weight)


def solution(mesh):
    return jax.shard_map(
        body,
        mesh=mesh,
        in_specs=(
            P(("rep", "exp", "tp"), None),
            P(("rep", "exp", "tp"), None),
            P(("rep", "exp", "tp"), None),
            P("exp", None, "tp"),
            P("exp", None, "tp"),
            P("exp", "tp", None),
        ),
        out_specs=P(("rep", "exp", "tp"), None),
        check_vma=False,
    )
```

```python
import functools

import jax
import jax.numpy as jnp
from jax import lax
from jax.experimental import pallas as pl
from jax.experimental.pallas import tpu as pltpu
from jax.sharding import PartitionSpec as P

MESH = pl.DeviceIdType.MESH
LANES = 128
VMEM_BYTES = 62000000


def kernel(
    dims, cw, pieces, early,
    ids_hbm, gates_hbm, tok_hbm, gw_ref, uw_ref, dw_ref, out_ref,
    ids_ref, gates_ref, xg, stage, x, wst, acc, h, wbuf, dbuf, keep,
    ex_send, ex_recv, q_send, q_recv, f_send, f_recv,
    in_sem, gu_sem, dn_sem, g_send, z_recv, g_recv, e_recv,
    s_send, ex_rsem, q_rsem, f_rsem,
):
    nr, ny, nz, own = dims
    nq = nr * ny
    r = lax.axis_index("rep")
    e = lax.axis_index("exp")
    t = lax.axis_index("tp")
    z, q = t // ny, r * ny + t % ny
    other = 1 - e
    rows, width = tok_hbm.shape
    hidden = gw_ref.shape[2]
    experts = gw_ref.shape[0]
    tokens = x.shape[0]
    half = tokens // 2
    part = half // nq
    nc = width // cw
    spans = [slice(low * width // pieces[-1], high * width // pieces[-1]) for low, high in zip(pieces, pieces[1:])]
    pieces = len(spans)
    group = stage.shape[0] // rows
    nqz = nq * nz

    def slot_of(ee, qq, zz):
        return (ee * nz + zz) * nq + qq

    def device(qq, zz):
        return {"rep": qq // ny, "tp": zz * ny + qq % ny}

    a, b = q // ny + e * (q % ny - q // ny), q % ny + e * (q // ny - q % ny)

    def crossed(aa, bb):
        return aa * (ny + e * (1 - ny)) + bb * (1 + e * (ny - 1))

    def near(i):
        m = jnp.minimum(z, nz - 1 - z)
        both = (1 - 2 * ((i + 1) % 2)) * ((i + 1) // 2)
        one = jnp.where(z < nz - 1 - z, 1, -1) * (i - m)
        return z + jnp.where(i <= 2 * m, both, one)

    me = slot_of(e, q, z)

    barrier = pltpu.get_barrier_semaphore()
    greeted = 0

    def greet(device_id):
        pl.semaphore_signal(barrier, inc=1, device_id=device_id, device_id_type=MESH)

    for d in range(1, nz):
        greet(device(q, (z + d) % nz))
        greeted += 1
    for d in range(1, nq):
        greet(device((q + d) % nq, z))
        greeted += 1
    greet({"exp": other})
    greeted += 1

    def load_own():
        copies = [
            pltpu.make_async_copy(
                tok_hbm.at[:, span], xg.at[me, :, span], in_sem.at[2 + p]
            )
            for p, span in enumerate(spans)
        ]
        copies.append(pltpu.make_async_copy(ids_hbm, ids_ref, in_sem.at[0]))
        copies.append(pltpu.make_async_copy(gates_hbm, gates_ref, in_sem.at[1]))
        return copies

    for copy in load_own():
        copy.start()

    def gu_copies(p):
        return [
            pltpu.make_async_copy(
                ref.at[r * own + l, spans[p], :],
                wbuf.at[l, m, spans[p], :],
                gu_sem.at[l, m, p],
            )
            for l in range(own)
            for m, ref in enumerate((gw_ref, uw_ref))
        ]

    def dn_copies(c):
        return [
            pltpu.make_async_copy(
                dw_ref.at[r * own + l, :, pl.ds(c * cw, cw)], dbuf.at[l, c], dn_sem.at[l, c]
            )
            for l in range(own)
        ]

    def gu_start(low, high):
        for p in range(low, min(high, pieces)):
            for copy in gu_copies(p):
                copy.start()

    def dn_start(low, high):
        for c in range(low, min(high, nc)):
            for copy in dn_copies(c):
                copy.start()

    ahead = max(1, pieces - 1)
    for copy in load_own():
        copy.wait()
    gu_start(0, ahead)
    lane = lax.broadcasted_iota(jnp.int32, (rows, LANES), 1)
    same = (
        lax.broadcasted_iota(jnp.int32, (rows, rows), 0)
        == lax.broadcasted_iota(jnp.int32, (rows, rows), 1)
    )
    weight = jnp.zeros((rows, LANES), jnp.float32)
    for k in range(ids_ref.shape[0]):
        ids, gates = (
            jnp.sum(
                jnp.where(same, jnp.broadcast_to(ref[k:k + 1, :].astype(jnp.float32), (rows, rows)), 0.0),
                axis=1, keepdims=True,
            )
            for ref in (ids_ref, gates_ref)
        )
        weight += jnp.where(lane.astype(jnp.float32) == ids, gates * (1.0 / 256.0), 0.0)
    xg[me, :, width:] = weight.astype(jnp.bfloat16)

    pl.semaphore_wait(barrier, greeted)

    def send(p, slot, count, send_sem, recv_sem, device_id):
        span = slice(spans[p].start, width + LANES) if p == pieces - 1 else spans[p]
        blocks = xg.at[pl.ds(slot, count), :, span]
        return pltpu.make_async_remote_copy(
            src_ref=blocks, dst_ref=blocks, send_sem=send_sem, recv_sem=recv_sem,
            device_id=device_id, device_id_type=MESH,
        )

    def z_copy(p, d, count=1):
        return send(
            p, me, count, g_send.at[0, p], z_recv.at[p, z], device(q, (z + d) % nz)
        )

    def q_copy(p, zz, d):
        return send(
            p, slot_of(e, q, zz), 1, g_send.at[1, p], g_recv.at[p, zz],
            device((q + d) % nq, z),
        )

    def e_copy(p, zz):
        return send(
            p, slot_of(e, 0, zz), nq, g_send.at[2, p], e_recv.at[p], {"exp": other}
        )

    def await_z(p, zz):
        send(p, 0, 1, g_send.at[0, p], z_recv.at[p, zz], {"exp": other}).wait_recv()

    def await_q(p, zz):
        send(p, 0, nq - 1, g_send.at[1, p], g_recv.at[p, zz], {"exp": other}).wait_recv()

    def await_e(p):
        send(p, 0, nqz, g_send.at[2, p], e_recv.at[p], {"exp": other}).wait_recv()

    def gather_drain():
        for p in range(pieces):
            for i, count in enumerate((nz - 1, (nq - 1) * nz, nqz)):
                send(p, 0, count, g_send.at[i, p], e_recv.at[p], {"exp": other}).wait_send()

    def pass_q(p, zz):
        for d in range(1, nq):
            q_copy(p, zz, d).start()

    def z_start(p):
        for d in range(1, nz):
            z_copy(p, d).start()

    def z_relay(p):
        def go(i, carry):
            zz = near(i)
            await_z(p, zz)
            pass_q(p, zz)
            return carry

        lax.fori_loop(1, nz, go, 0)

    def q_relay(p, low, high):
        def go(i, carry):
            zz = jnp.where(i == 0, z, near(i))
            await_q(p, zz)
            e_copy(p, zz).start()
            return carry

        lax.fori_loop(low, high, go, 0)

    z_start(0)
    pass_q(0, z)
    for p in range(1, pieces):
        z_start(p)

    def lay(p, side):
        low, high = spans[p].start, spans[p].stop + (LANES if p == pieces - 1 else 0)

        def go(g, carry):
            for i in range(group):
                place = g * group + i
                slot = slot_of(side, place // nz, place % nz)
                stage[i * rows:(i + 1) * rows, low:high] = xg[slot, :, low:high].astype(jnp.float32)
            r0 = pl.multiple_of(side * half + g * group * rows, group * rows)
            x[pl.ds(r0, group * rows), spans[p]] = stage[:, spans[p]].astype(jnp.bfloat16)
            if p == pieces - 1:
                wst[pl.ds(r0, group * rows), :] = stage[:, width:]
            return carry

        lax.fori_loop(0, half // (group * rows), go, 0)

    step = 256

    def project(p):
        for copy in gu_copies(p):
            copy.wait()
        for l in range(own):
            for n in range(0, hidden, step):
                cols = slice(n, min(n + step, hidden))
                gate, upper = (
                    jnp.dot(
                        x[:, spans[p]], wbuf[l, m, spans[p], cols],
                        preferred_element_type=jnp.float32,
                    )
                    for m in range(2)
                )
                if p > 0:
                    gate = gate + acc[l, 0, :, cols]
                    upper = upper + acc[l, 1, :, cols]
                if p < pieces - 1:
                    acc[l, 0, :, cols] = gate
                    acc[l, 1, :, cols] = upper
                else:
                    h[l, :, cols] = (gate / (1.0 + jnp.exp(-gate)) * upper).astype(jnp.bfloat16)

    for p in range(pieces):
        z_relay(p)
        if p == 0:
            gu_start(ahead, pieces)
            dn_start(0, 2)
        if p + 1 < pieces:
            pass_q(p + 1, z)
    q_relay(0, 0, nz)
    dn_start(2, nc)
    for p in range(pieces):
        lay(p, e)
        if p + 1 < pieces:
            q_relay(p + 1, 0, nz)
        await_e(p)
        lay(p, other)
        project(p)

    lanes = lax.broadcasted_iota(jnp.int32, (tokens, LANES), 1)
    first = e * experts + r * own
    scales = [
        jnp.sum(jnp.where(lanes == first + l, wst[...], 0.0), axis=1, keepdims=True)
        for l in range(own)
    ]

    def ex_copy(c):
        return pltpu.make_async_remote_copy(
            src_ref=ex_send.at[c], dst_ref=ex_recv.at[c],
            send_sem=s_send.at[0], recv_sem=ex_rsem.at[c],
            device_id={"exp": other}, device_id_type=MESH,
        )

    def sq_copies(c):
        if c < early:
            pairs = [
                (crossed((a + d) % nr, i), d * nr + i, crossed((a + d) % nr, b))
                for d in range(1, nr)
                for i in range(nr)
            ]
        else:
            pairs = [((q + d) % nq, d, (q + d) % nq) for d in range(1, nq)]
        return [
            pltpu.make_async_remote_copy(
                src_ref=q_send.at[c, block], dst_ref=q_recv.at[c, place],
                send_sem=s_send.at[1], recv_sem=q_rsem.at[c],
                device_id=device(target, z), device_id_type=MESH,
            )
            for block, place, target in pairs
        ]

    def f_copy(c, d):
        if c < early:
            place = (b * nz + z + d) % (nr * nz)
            target = device(crossed(a, place // nz), place % nz)
        else:
            place = (z + d) % nz
            target = device(q, place)
        return pltpu.make_async_remote_copy(
            src_ref=f_send.at[c, place], dst_ref=f_recv.at[c, d],
            send_sem=s_send.at[2], recv_sem=f_rsem.at[c],
            device_id=target, device_id_type=MESH,
        )

    def q_count(c):
        return (nr - 1) * nr if c < early else nq - 1

    def f_count(c):
        return nr * nz if c < early else nz

    def some(buffer, c, count, i, recv_sem):
        blocks = buffer.at[c, pl.ds(0, count)]
        return pltpu.make_async_remote_copy(
            src_ref=blocks, dst_ref=blocks, send_sem=s_send.at[i], recv_sem=recv_sem.at[c],
            device_id={"exp": other}, device_id_type=MESH,
        )

    def sum_drain(low, high):
        for c in range(low, high):
            ex_copy(c).wait_send()
            some(q_send, c, q_count(c), 1, q_rsem).wait_send()
            some(f_send, c, f_count(c) - 1, 2, f_rsem).wait_send()

    def down(chunks):
        for c in chunks:
            for copy in dn_copies(c):
                copy.wait()
        for c in chunks:
            for n in range(0, cw, step):
                cols = slice(n, min(n + step, cw))
                total = None
                for l in range(own):
                    value = scales[l] * jnp.dot(
                        h[l], dbuf[l, c, :, cols], preferred_element_type=jnp.float32
                    )
                    total = value if total is None else total + value
                low, high = total[:half], total[half:]
                keep[c, :, cols] = jnp.where(e == 0, low, high)
                ex_send[c, :, cols] = jnp.where(e == 0, high, low).astype(jnp.bfloat16)
        for c in chunks:
            ex_copy(c).start()

    def pass_ex(c):
        ex_copy(c).wait_recv()
        for qq in range(nq):
            span = slice(qq * part, (qq + 1) * part)
            total = keep[c, span, :] + ex_recv[c, span, :].astype(jnp.float32)
            q_send[c, qq] = total.astype(jnp.bfloat16)
            keep[c, span, :] = total
        for copy in sq_copies(c):
            copy.start()

    def kept(c, block):
        return keep[c, pl.ds(pl.multiple_of(block * part, part), part), :]

    def pass_q_sum(c):
        some(q_recv, c, q_count(c), 1, q_rsem).wait_recv()
        if c < early:
            sums = [
                sum(
                    (q_recv[c, d * nr + i].astype(jnp.float32) for d in range(1, nr)),
                    start=kept(c, crossed(a, i)),
                )
                for i in range(nr)
            ]
            mine = b * nz + z
        else:
            sums = [
                sum((q_recv[c, d].astype(jnp.float32) for d in range(1, nq)), start=kept(c, q))
            ]
            mine = z
        for i, total in enumerate(sums):
            for j in range(nz):
                f_send[c, i * nz + j] = total[j * rows:(j + 1) * rows, :].astype(jnp.bfloat16)
        f_recv[c, 0] = f_send[c, mine]
        for d in range(1, f_count(c)):
            f_copy(c, d).start()

    def collect(c):
        some(f_recv, c, f_count(c) - 1, 2, f_rsem).wait_recv()
        total = f_recv[c, 0].astype(jnp.float32)
        for d in range(1, f_count(c)):
            total += f_recv[c, d].astype(jnp.float32)
        out_ref[:, c * cw:(c + 1) * cw] = total.astype(out_ref.dtype)

    groups = [range(c, min(c + 2, nc)) for c in range(0, nc, 2)]
    for i, chunks in enumerate(groups):
        down(chunks)
        if i >= 2:
            for c in groups[i - 2]:
                pass_ex(c)
    gather_drain()
    for chunks in groups[-2:]:
        for c in chunks:
            pass_ex(c)
    for c in range(nc):
        pass_q_sum(c)
    for c in range(nc):
        if c == nc - 1:
            sum_drain(0, nc - 1)
        collect(c)
    sum_drain(nc - 1, nc)


def body(tokens, expert_ids, gate_ints, gate_weight, up_weight, down_weight):
    rows, width = tokens.shape
    experts, _, hidden = gate_weight.shape
    nt = lax.axis_size("tp")
    nr = lax.axis_size("rep")
    ny = 1
    while nt % (ny * 2) == 0 and (ny * 2) ** 2 <= nt:
        ny *= 2
    nz = nt // ny
    assert experts % nr == 0 and lax.axis_size("exp") == 2
    own = experts // nr
    slots = nt * nr * 2
    total = slots * rows
    cuts = (0, 1, 2, 4)
    pieces = len(cuts) - 1
    cw = min(512, width)
    nc = width // cw
    early = nc // 2 if nr == ny else 0
    ends = nt if early else nz
    bf16, f32, i32 = jnp.bfloat16, jnp.float32, jnp.int32
    vmem = pl.BlockSpec(memory_space=pltpu.VMEM)
    hbm = pl.BlockSpec(memory_space=pl.ANY)
    dma = pltpu.SemaphoreType.DMA
    nq = nr * ny
    part = total // 2 // nq
    top = expert_ids.shape[1]
    return pl.pallas_call(
        functools.partial(kernel, (nr, ny, nz, own), cw, cuts, early),
        out_shape=pltpu.VMEM((rows, width), bf16),
        in_specs=[hbm] * 6,
        out_specs=vmem,
        scratch_shapes=[
            pltpu.VMEM((top, rows), i32),
            pltpu.VMEM((top, rows), i32),
            pltpu.VMEM((slots, rows, width + LANES), bf16),
            pltpu.VMEM((16, width + LANES), f32),
            pltpu.VMEM((total, width), bf16),
            pltpu.VMEM((total, LANES), f32),
            pltpu.VMEM((own, 2, total, hidden), f32),
            pltpu.VMEM((own, total, hidden), bf16),
            pltpu.VMEM((own, 2, width, hidden), bf16),
            pltpu.VMEM((own, nc, hidden, cw), bf16),
            pltpu.VMEM((nc, total // 2, cw), f32),
            pltpu.VMEM((nc, total // 2, cw), bf16),
            pltpu.VMEM((nc, total // 2, cw), bf16),
            pltpu.VMEM((nc, nq, part, cw), bf16),
            pltpu.VMEM((nc, nq, part, cw), bf16),
            pltpu.VMEM((nc, ends, rows, cw), bf16),
            pltpu.VMEM((nc, ends, rows, cw), bf16),
            dma((2 + pieces,)),
            dma((own, 2, pieces)),
            dma((own, nc)),
            dma((3, pieces)),
            dma((pieces, nz)),
            dma((pieces, nz)),
            dma((pieces,)),
            dma((3,)),
            dma((nc,)),
            dma((nc,)),
            dma((nc,)),
        ],
        compiler_params=pltpu.CompilerParams(
            collective_id=0, has_side_effects=True, vmem_limit_bytes=VMEM_BYTES
        ),
    )(expert_ids.T, gate_ints.T, tokens, gate_weight, up_weight, down_weight)


def solution(mesh):
    return jax.shard_map(
        body,
        mesh=mesh,
        in_specs=(
            P(("rep", "exp", "tp"), None),
            P(("rep", "exp", "tp"), None),
            P(("rep", "exp", "tp"), None),
            P("exp", None, "tp"),
            P("exp", None, "tp"),
            P("exp", "tp", None),
        ),
        out_specs=P(("rep", "exp", "tp"), None),
        check_vma=False,
    )
```

```python
import functools

import jax
import jax.numpy as jnp
from jax import lax
from jax.experimental import pallas as pl
from jax.experimental.pallas import tpu as pltpu
from jax.sharding import PartitionSpec as P

MESH = pl.DeviceIdType.MESH
LANES = 128
VMEM_BYTES = 62000000


def kernel(
    dims, cw, pieces, early,
    ids_hbm, gates_hbm, tok_hbm, gw_ref, uw_ref, dw_ref, out_ref,
    ids_ref, gates_ref, xg, stage, x, wst, acc, h, wbuf, dbuf, keep,
    ex_send, ex_recv, q_send, q_recv, f_send, f_recv,
    in_sem, gu_sem, dn_sem, g_send, z_recv, g_recv, e_recv,
    s_send, ex_rsem, q_rsem, f_rsem,
):
    nr, ny, nz, own = dims
    nq = nr * ny
    r = lax.axis_index("rep")
    e = lax.axis_index("exp")
    t = lax.axis_index("tp")
    z, q = t // ny, r * ny + t % ny
    other = 1 - e
    rows, width = tok_hbm.shape
    hidden = gw_ref.shape[2]
    experts = gw_ref.shape[0]
    tokens = x.shape[0]
    half = tokens // 2
    part = half // nq
    nc = width // cw
    spans = [slice(low * width // pieces[-1], high * width // pieces[-1]) for low, high in zip(pieces, pieces[1:])]
    pieces = len(spans)
    group = stage.shape[0] // rows
    nqz = nq * nz

    def slot_of(ee, qq, zz):
        return (ee * nz + zz) * nq + qq

    def device(qq, zz):
        return {"rep": qq // ny, "tp": zz * ny + qq % ny}

    a, b = q // ny + e * (q % ny - q // ny), q % ny + e * (q // ny - q % ny)

    def crossed(aa, bb):
        return aa * (ny + e * (1 - ny)) + bb * (1 + e * (ny - 1))

    def near(i):
        m = jnp.minimum(z, nz - 1 - z)
        both = (1 - 2 * ((i + 1) % 2)) * ((i + 1) // 2)
        one = jnp.where(z < nz - 1 - z, 1, -1) * (i - m)
        return z + jnp.where(i <= 2 * m, both, one)

    me = slot_of(e, q, z)

    barrier = pltpu.get_barrier_semaphore()
    greeted = 0

    def greet(device_id):
        pl.semaphore_signal(barrier, inc=1, device_id=device_id, device_id_type=MESH)

    for d in range(1, nz):
        greet(device(q, (z + d) % nz))
        greeted += 1
    for d in range(1, nq):
        greet(device((q + d) % nq, z))
        greeted += 1
    greet({"exp": other})
    greeted += 1

    def load_own():
        copies = [
            pltpu.make_async_copy(
                tok_hbm.at[:, span], xg.at[me, :, span], in_sem.at[2 + p]
            )
            for p, span in enumerate(spans)
        ]
        copies.append(pltpu.make_async_copy(ids_hbm, ids_ref, in_sem.at[0]))
        copies.append(pltpu.make_async_copy(gates_hbm, gates_ref, in_sem.at[1]))
        return copies

    for copy in load_own():
        copy.start()

    def gu_copies(p):
        return [
            pltpu.make_async_copy(
                ref.at[r * own + l, spans[p], :],
                wbuf.at[l, m, spans[p], :],
                gu_sem.at[l, p],
            )
            for l in range(own)
            for m, ref in enumerate((gw_ref, uw_ref))
        ]

    def dn_copies(c):
        return [
            pltpu.make_async_copy(
                dw_ref.at[r * own + l, :, pl.ds(c * cw, cw)], dbuf.at[l, c], dn_sem.at[l, c // 2]
            )
            for l in range(own)
        ]

    def gu_start(low, high):
        for p in range(low, min(high, pieces)):
            for copy in gu_copies(p):
                copy.start()

    def dn_start(low, high):
        for c in range(low, min(high, nc)):
            for copy in dn_copies(c):
                copy.start()

    ahead = max(1, pieces - 1)
    for copy in load_own():
        copy.wait()
    gu_start(0, ahead)
    pl.semaphore_wait(barrier, greeted)

    def send(p, slot, count, send_sem, recv_sem, device_id):
        span = slice(spans[p].start, width + LANES) if p == pieces - 1 else spans[p]
        blocks = xg.at[pl.ds(slot, count), :, span]
        return pltpu.make_async_remote_copy(
            src_ref=blocks, dst_ref=blocks, send_sem=send_sem, recv_sem=recv_sem,
            device_id=device_id, device_id_type=MESH,
        )

    def z_copy(p, d, count=1):
        return send(
            p, me, count, g_send.at[0], z_recv.at[p, z], device(q, (z + d) % nz)
        )

    def q_copy(p, zz, d):
        return send(
            p, slot_of(e, q, zz), 1, g_send.at[1], g_recv.at[p, zz],
            device((q + d) % nq, z),
        )

    def e_copy(p, zz):
        return send(
            p, slot_of(e, 0, zz), nq, g_send.at[2], e_recv.at[p], {"exp": other}
        )

    def await_z(p, zz):
        send(p, 0, 1, g_send.at[0], z_recv.at[p, zz], {"exp": other}).wait_recv()

    def await_q(p, zz):
        send(p, 0, nq - 1, g_send.at[1], g_recv.at[p, zz], {"exp": other}).wait_recv()

    def await_e(p):
        send(p, 0, nqz, g_send.at[2], e_recv.at[p], {"exp": other}).wait_recv()

    def gather_drain():
        for i, count in enumerate((nz - 1, (nq - 1) * nz, nqz)):
            whole = xg.at[pl.ds(0, count)]
            pltpu.make_async_remote_copy(
                src_ref=whole, dst_ref=whole, send_sem=g_send.at[i], recv_sem=e_recv.at[0],
                device_id={"exp": other}, device_id_type=MESH,
            ).wait_send()

    def pass_q(p, zz):
        for d in range(1, nq):
            q_copy(p, zz, d).start()

    def z_start(p):
        for d in range(1, nz):
            z_copy(p, d).start()

    def z_relay(p):
        def go(i, carry):
            zz = near(i)
            await_z(p, zz)
            pass_q(p, zz)
            return carry

        lax.fori_loop(1, nz, go, 0)

    def q_relay(p, low, high):
        def go(i, carry):
            zz = jnp.where(i == 0, z, near(i))
            await_q(p, zz)
            e_copy(p, zz).start()
            return carry

        lax.fori_loop(low, high, go, 0)

    z_start(0)
    pass_q(0, z)
    lane = lax.broadcasted_iota(jnp.int32, (rows, LANES), 1)
    same = (
        lax.broadcasted_iota(jnp.int32, (rows, rows), 0)
        == lax.broadcasted_iota(jnp.int32, (rows, rows), 1)
    )
    weight = jnp.zeros((rows, LANES), jnp.float32)
    for k in range(ids_ref.shape[0]):
        ids, gates = (
            jnp.sum(
                jnp.where(same, jnp.broadcast_to(ref[k:k + 1, :].astype(jnp.float32), (rows, rows)), 0.0),
                axis=1, keepdims=True,
            )
            for ref in (ids_ref, gates_ref)
        )
        weight += jnp.where(lane.astype(jnp.float32) == ids, gates * (1.0 / 256.0), 0.0)
    xg[me, :, width:] = weight.astype(jnp.bfloat16)
    for p in range(1, pieces):
        z_start(p)

    def lay(p, side):
        low, high = spans[p].start, spans[p].stop + (LANES if p == pieces - 1 else 0)

        def go(g, carry):
            for i in range(group):
                place = g * group + i
                slot = slot_of(side, place // nz, place % nz)
                stage[i * rows:(i + 1) * rows, low:high] = xg[slot, :, low:high].astype(jnp.float32)
            r0 = pl.multiple_of(side * half + g * group * rows, group * rows)
            x[pl.ds(r0, group * rows), spans[p]] = stage[:, spans[p]].astype(jnp.bfloat16)
            if p == pieces - 1:
                wst[pl.ds(r0, group * rows), :] = stage[:, width:]
            return carry

        steps = half // (group * rows)
        if steps > 8:
            lax.fori_loop(0, steps, go, 0)
        else:
            for g in range(steps):
                go(g, 0)

    step = 256

    def project(p):
        for l in range(own):
            both = wbuf.at[l, :, spans[p], :]
            pltpu.make_async_copy(both, both, gu_sem.at[l, p]).wait()
        for l in range(own):
            for n in range(0, hidden, step):
                cols = slice(n, min(n + step, hidden))
                gate, upper = (
                    jnp.dot(
                        x[:, spans[p]], wbuf[l, m, spans[p], cols],
                        preferred_element_type=jnp.float32,
                    )
                    for m in range(2)
                )
                if p > 0:
                    gate = gate + acc[l, 0, :, cols]
                    upper = upper + acc[l, 1, :, cols]
                if p < pieces - 1:
                    acc[l, 0, :, cols] = gate
                    acc[l, 1, :, cols] = upper
                else:
                    h[l, :, cols] = (gate / (1.0 + jnp.exp(-gate)) * upper).astype(jnp.bfloat16)

    for p in range(pieces):
        z_relay(p)
        if p == 0:
            gu_start(ahead, pieces)
            dn_start(0, 2)
        if p + 1 < pieces:
            pass_q(p + 1, z)
    q_relay(0, 0, nz)
    dn_start(2, nc)
    lay(0, e)
    for p in range(pieces):
        if p + 1 < pieces:
            q_relay(p + 1, 0, nz)
        await_e(p)
        lay(p, other)
        if p + 1 < pieces:
            lay(p + 1, e)
        project(p)

    lanes = lax.broadcasted_iota(jnp.int32, (tokens, LANES), 1)
    first = e * experts + r * own
    scales = [
        jnp.sum(jnp.where(lanes == first + l, wst[...], 0.0), axis=1, keepdims=True)
        for l in range(own)
    ]

    def ex_copy(c):
        return pltpu.make_async_remote_copy(
            src_ref=ex_send.at[c], dst_ref=ex_recv.at[c],
            send_sem=s_send.at[0], recv_sem=ex_rsem.at[c // 2],
            device_id={"exp": other}, device_id_type=MESH,
        )

    def sq_copies(c):
        if c < early:
            pairs = [
                (crossed((a + d) % nr, i), d * nr + i, crossed((a + d) % nr, b))
                for d in range(1, nr)
                for i in range(nr)
            ]
        else:
            pairs = [((q + d) % nq, d, (q + d) % nq) for d in range(1, nq)]
        return [
            pltpu.make_async_remote_copy(
                src_ref=q_send.at[c, block], dst_ref=q_recv.at[c, place],
                send_sem=s_send.at[1], recv_sem=q_rsem.at[c],
                device_id=device(target, z), device_id_type=MESH,
            )
            for block, place, target in pairs
        ]

    def f_copy(c, d):
        if c < early:
            place = (b * nz + z + d) % (nr * nz)
            target = device(crossed(a, place // nz), place % nz)
        else:
            place = (z + d) % nz
            target = device(q, place)
        return pltpu.make_async_remote_copy(
            src_ref=f_send.at[c, place], dst_ref=f_recv.at[c, d],
            send_sem=s_send.at[2], recv_sem=f_rsem.at[c],
            device_id=target, device_id_type=MESH,
        )

    def q_count(c):
        return (nr - 1) * nr if c < early else nq - 1

    def f_count(c):
        return nr * nz if c < early else nz

    def some(buffer, c, count, i, recv_sem):
        blocks = buffer.at[c, pl.ds(0, count)]
        return pltpu.make_async_remote_copy(
            src_ref=blocks, dst_ref=blocks, send_sem=s_send.at[i], recv_sem=recv_sem.at[c],
            device_id={"exp": other}, device_id_type=MESH,
        )

    def sum_drain(low, high):
        for c in range(low, high):
            ex_copy(c).wait_send()
            some(q_send, c, q_count(c), 1, q_rsem).wait_send()
            some(f_send, c, f_count(c) - 1, 2, f_rsem).wait_send()

    def down(chunks):
        for l in range(own):
            both = dbuf.at[l, pl.ds(chunks[0], len(chunks))]
            pltpu.make_async_copy(both, both, dn_sem.at[l, chunks[0] // 2]).wait()
        for c in chunks:
            for n in range(0, cw, step):
                cols = slice(n, min(n + step, cw))
                total = None
                for l in range(own):
                    value = scales[l] * jnp.dot(
                        h[l], dbuf[l, c, :, cols], preferred_element_type=jnp.float32
                    )
                    total = value if total is None else total + value
                low, high = total[:half], total[half:]
                keep[c, :, cols] = jnp.where(e == 0, low, high)
                ex_send[c, :, cols] = jnp.where(e == 0, high, low).astype(jnp.bfloat16)
        for c in chunks:
            ex_copy(c).start()

    def await_ex(chunks):
        blocks = ex_recv.at[pl.ds(chunks[0], len(chunks))]
        pltpu.make_async_remote_copy(
            src_ref=blocks, dst_ref=blocks, send_sem=s_send.at[0],
            recv_sem=ex_rsem.at[chunks[0] // 2], device_id={"exp": other}, device_id_type=MESH,
        ).wait_recv()

    def pass_ex(c):
        for qq in range(nq):
            span = slice(qq * part, (qq + 1) * part)
            total = keep[c, span, :] + ex_recv[c, span, :].astype(jnp.float32)
            q_send[c, qq] = total.astype(jnp.bfloat16)
            keep[c, span, :] = total
        for copy in sq_copies(c):
            copy.start()

    def kept(c, block):
        return keep[c, pl.ds(pl.multiple_of(block * part, part), part), :]

    def pass_q_sum(c):
        some(q_recv, c, q_count(c), 1, q_rsem).wait_recv()
        if c < early:
            sums = [
                sum(
                    (q_recv[c, d * nr + i].astype(jnp.float32) for d in range(1, nr)),
                    start=kept(c, crossed(a, i)),
                )
                for i in range(nr)
            ]
            mine = b * nz + z
        else:
            sums = [
                sum((q_recv[c, d].astype(jnp.float32) for d in range(1, nq)), start=kept(c, q))
            ]
            mine = z
        for i, total in enumerate(sums):
            for j in range(nz):
                f_send[c, i * nz + j] = total[j * rows:(j + 1) * rows, :].astype(jnp.bfloat16)
        f_recv[c, 0] = f_send[c, mine]
        for d in range(1, f_count(c)):
            f_copy(c, d).start()

    def collect(c):
        some(f_recv, c, f_count(c) - 1, 2, f_rsem).wait_recv()
        total = f_recv[c, 0].astype(jnp.float32)
        for d in range(1, f_count(c)):
            total += f_recv[c, d].astype(jnp.float32)
        out_ref[:, c * cw:(c + 1) * cw] = total.astype(out_ref.dtype)

    groups = [range(c, min(c + 2, nc)) for c in range(0, nc, 2)]
    for i, chunks in enumerate(groups):
        down(chunks)
        if i >= 2:
            await_ex(groups[i - 2])
            for c in groups[i - 2]:
                pass_ex(c)
    gather_drain()
    for chunks in groups[-2:]:
        await_ex(chunks)
        for c in chunks:
            pass_ex(c)
    for c in range(nc):
        pass_q_sum(c)
    for c in range(nc):
        if c == nc - 1:
            sum_drain(0, nc - 1)
        collect(c)
    sum_drain(nc - 1, nc)


def body(tokens, expert_ids, gate_ints, gate_weight, up_weight, down_weight):
    rows, width = tokens.shape
    experts, _, hidden = gate_weight.shape
    nt = lax.axis_size("tp")
    nr = lax.axis_size("rep")
    ny = 1
    while nt % (ny * 2) == 0 and (ny * 2) ** 2 <= nt:
        ny *= 2
    nz = nt // ny
    assert experts % nr == 0 and lax.axis_size("exp") == 2
    own = experts // nr
    slots = nt * nr * 2
    total = slots * rows
    cuts = (0, 1, 2, 4)
    pieces = len(cuts) - 1
    cw = min(512, width)
    nc = width // cw
    early = nc // 2 if nr == ny else 0
    ends = nt if early else nz
    bf16, f32, i32 = jnp.bfloat16, jnp.float32, jnp.int32
    vmem = pl.BlockSpec(memory_space=pltpu.VMEM)
    hbm = pl.BlockSpec(memory_space=pl.ANY)
    dma = pltpu.SemaphoreType.DMA
    nq = nr * ny
    part = total // 2 // nq
    top = expert_ids.shape[1]
    return pl.pallas_call(
        functools.partial(kernel, (nr, ny, nz, own), cw, cuts, early),
        out_shape=pltpu.VMEM((rows, width), bf16),
        in_specs=[hbm] * 6,
        out_specs=vmem,
        scratch_shapes=[
            pltpu.VMEM((top, rows), i32),
            pltpu.VMEM((top, rows), i32),
            pltpu.VMEM((slots, rows, width + LANES), bf16),
            pltpu.VMEM((16, width + LANES), f32),
            pltpu.VMEM((total, width), bf16),
            pltpu.VMEM((total, LANES), f32),
            pltpu.VMEM((own, 2, total, hidden), f32),
            pltpu.VMEM((own, total, hidden), bf16),
            pltpu.VMEM((own, 2, width, hidden), bf16),
            pltpu.VMEM((own, nc, hidden, cw), bf16),
            pltpu.VMEM((nc, total // 2, cw), f32),
            pltpu.VMEM((nc, total // 2, cw), bf16),
            pltpu.VMEM((nc, total // 2, cw), bf16),
            pltpu.VMEM((nc, nq, part, cw), bf16),
            pltpu.VMEM((nc, nq, part, cw), bf16),
            pltpu.VMEM((nc, ends, rows, cw), bf16),
            pltpu.VMEM((nc, ends, rows, cw), bf16),
            dma((2 + pieces,)),
            dma((own, pieces)),
            dma((own, -(-nc // 2))),
            dma((3,)),
            dma((pieces, nz)),
            dma((pieces, nz)),
            dma((pieces,)),
            dma((3,)),
            dma((-(-nc // 2),)),
            dma((nc,)),
            dma((nc,)),
        ],
        compiler_params=pltpu.CompilerParams(
            collective_id=0, has_side_effects=True, vmem_limit_bytes=VMEM_BYTES
        ),
    )(expert_ids.T, gate_ints.T, tokens, gate_weight, up_weight, down_weight)


def solution(mesh):
    return jax.shard_map(
        body,
        mesh=mesh,
        in_specs=(
            P(("rep", "exp", "tp"), None),
            P(("rep", "exp", "tp"), None),
            P(("rep", "exp", "tp"), None),
            P("exp", None, "tp"),
            P("exp", None, "tp"),
            P("exp", "tp", None),
        ),
        out_specs=P(("rep", "exp", "tp"), None),
        check_vma=False,
    )
```

```python
import functools

import jax
import jax.numpy as jnp
from jax import lax
from jax.experimental import pallas as pl
from jax.experimental.pallas import tpu as pltpu
from jax.sharding import PartitionSpec as P

MESH = pl.DeviceIdType.MESH
LANES = 128
VMEM_BYTES = 62000000


def kernel(
    dims, cw, pieces, early,
    ids_hbm, gates_hbm, tok_hbm, gw_ref, uw_ref, dw_ref, out_ref,
    ids_ref, gates_ref, xg, stage, x, wst, acc, h, wbuf, dbuf, keep,
    ex_send, ex_recv, q_send, q_recv, f_send, f_recv,
    in_sem, gu_sem, dn_sem, g_send, z_recv, g_recv, e_recv,
    s_send, ex_rsem, q_rsem, f_rsem,
):
    nr, ny, nz, own = dims
    nq = nr * ny
    r = lax.axis_index("rep")
    e = lax.axis_index("exp")
    t = lax.axis_index("tp")
    z, q = t // ny, r * ny + t % ny
    other = 1 - e
    rows, width = tok_hbm.shape
    hidden = gw_ref.shape[2]
    experts = gw_ref.shape[0]
    tokens = x.shape[0]
    half = tokens // 2
    part = half // nq
    nc = width // cw
    spans = [slice(low * width // pieces[-1], high * width // pieces[-1]) for low, high in zip(pieces, pieces[1:])]
    pieces = len(spans)
    group = stage.shape[0] // rows
    nqz = nq * nz

    def slot_of(ee, qq, zz):
        return (ee * nz + zz) * nq + qq

    def device(qq, zz):
        return {"rep": qq // ny, "tp": zz * ny + qq % ny}

    a, b = q // ny + e * (q % ny - q // ny), q % ny + e * (q // ny - q % ny)

    def crossed(aa, bb):
        return aa * (ny + e * (1 - ny)) + bb * (1 + e * (ny - 1))

    def near(i):
        m = jnp.minimum(z, nz - 1 - z)
        both = (1 - 2 * ((i + 1) % 2)) * ((i + 1) // 2)
        one = jnp.where(z < nz - 1 - z, 1, -1) * (i - m)
        return z + jnp.where(i <= 2 * m, both, one)

    moves = sorted(
        ((dr, dy) for dr in range(nr) for dy in range(ny) if dr or dy),
        key=lambda move: -sum(i > 0 for i in move),
    )

    def moved(d):
        dr, dy = moves[d - 1]
        return (q // ny + dr) % nr * ny + (q % ny + dy) % ny

    me = slot_of(e, q, z)

    barrier = pltpu.get_barrier_semaphore()
    greeted = 0

    def greet(device_id):
        pl.semaphore_signal(barrier, inc=1, device_id=device_id, device_id_type=MESH)

    for d in range(1, nz):
        greet(device(q, (z + d) % nz))
        greeted += 1
    for d in range(1, nq):
        greet(device((q + d) % nq, z))
        greeted += 1
    greet({"exp": other})
    greeted += 1

    def load_own():
        copies = [
            pltpu.make_async_copy(
                tok_hbm.at[:, span], xg.at[me, :, span], in_sem.at[2 + p]
            )
            for p, span in enumerate(spans)
        ]
        copies.append(pltpu.make_async_copy(ids_hbm, ids_ref, in_sem.at[0]))
        copies.append(pltpu.make_async_copy(gates_hbm, gates_ref, in_sem.at[1]))
        return copies

    for copy in load_own():
        copy.start()

    def gu_copies(p):
        return [
            pltpu.make_async_copy(
                ref.at[r * own + l, spans[p], :],
                wbuf.at[l, m, spans[p], :],
                gu_sem.at[l, p],
            )
            for l in range(own)
            for m, ref in enumerate((gw_ref, uw_ref))
        ]

    def dn_copies(c):
        return [
            pltpu.make_async_copy(
                dw_ref.at[r * own + l, :, pl.ds(c * cw, cw)], dbuf.at[l, c], dn_sem.at[l, c // 2]
            )
            for l in range(own)
        ]

    def gu_start(low, high):
        for p in range(low, min(high, pieces)):
            for copy in gu_copies(p):
                copy.start()

    def dn_start(low, high):
        for c in range(low, min(high, nc)):
            for copy in dn_copies(c):
                copy.start()

    ahead = max(1, pieces - 1)
    for copy in load_own():
        copy.wait()
    gu_start(0, ahead)
    pl.semaphore_wait(barrier, greeted)

    def send(p, slot, count, send_sem, recv_sem, device_id):
        span = slice(spans[p].start, width + LANES) if p == pieces - 1 else spans[p]
        blocks = xg.at[pl.ds(slot, count), :, span]
        return pltpu.make_async_remote_copy(
            src_ref=blocks, dst_ref=blocks, send_sem=send_sem, recv_sem=recv_sem,
            device_id=device_id, device_id_type=MESH,
        )

    def z_copy(p, d, count=1):
        return send(
            p, me, count, g_send.at[0], z_recv.at[p, z], device(q, near(nz - d))
        )

    def q_copy(p, zz, d):
        return send(
            p, slot_of(e, q, zz), 1, g_send.at[1], g_recv.at[p, zz],
            device(moved(d), z),
        )

    def e_copy(p, zz):
        return send(
            p, slot_of(e, 0, zz), nq, g_send.at[2], e_recv.at[p], {"exp": other}
        )

    def await_z(p, zz):
        send(p, 0, 1, g_send.at[0], z_recv.at[p, zz], {"exp": other}).wait_recv()

    def await_q(p, zz):
        send(p, 0, nq - 1, g_send.at[1], g_recv.at[p, zz], {"exp": other}).wait_recv()

    def await_e(p):
        send(p, 0, nqz, g_send.at[2], e_recv.at[p], {"exp": other}).wait_recv()

    def gather_drain():
        for i, count in enumerate((nz - 1, (nq - 1) * nz, nqz)):
            whole = xg.at[pl.ds(0, count)]
            pltpu.make_async_remote_copy(
                src_ref=whole, dst_ref=whole, send_sem=g_send.at[i], recv_sem=e_recv.at[0],
                device_id={"exp": other}, device_id_type=MESH,
            ).wait_send()

    def pass_q(p, zz):
        for d in range(1, nq):
            q_copy(p, zz, d).start()

    def z_start(p):
        for d in range(1, nz):
            z_copy(p, d).start()

    def z_relay(p):
        def go(i, carry):
            zz = near(i)
            await_z(p, zz)
            pass_q(p, zz)
            return carry

        lax.fori_loop(1, nz, go, 0)

    def q_relay(p, low, high):
        def go(i, carry):
            zz = jnp.where(i == 0, z, near(i))
            await_q(p, zz)
            e_copy(p, zz).start()
            return carry

        lax.fori_loop(low, high, go, 0)

    z_start(0)
    pass_q(0, z)
    lane = lax.broadcasted_iota(jnp.int32, (rows, LANES), 1)
    same = (
        lax.broadcasted_iota(jnp.int32, (rows, rows), 0)
        == lax.broadcasted_iota(jnp.int32, (rows, rows), 1)
    )
    weight = jnp.zeros((rows, LANES), jnp.float32)
    for k in range(ids_ref.shape[0]):
        ids, gates = (
            jnp.sum(
                jnp.where(same, jnp.broadcast_to(ref[k:k + 1, :].astype(jnp.float32), (rows, rows)), 0.0),
                axis=1, keepdims=True,
            )
            for ref in (ids_ref, gates_ref)
        )
        weight += jnp.where(lane.astype(jnp.float32) == ids, gates * (1.0 / 256.0), 0.0)
    xg[me, :, width:] = weight.astype(jnp.bfloat16)
    for p in range(1, pieces):
        z_start(p)

    def lay(p, side):
        low, high = spans[p].start, spans[p].stop + (LANES if p == pieces - 1 else 0)

        def go(g, carry):
            for i in range(group):
                place = g * group + i
                slot = slot_of(side, place // nz, place % nz)
                stage[i * rows:(i + 1) * rows, low:high] = xg[slot, :, low:high].astype(jnp.float32)
            r0 = pl.multiple_of(side * half + g * group * rows, group * rows)
            x[pl.ds(r0, group * rows), spans[p]] = stage[:, spans[p]].astype(jnp.bfloat16)
            if p == pieces - 1:
                wst[pl.ds(r0, group * rows), :] = stage[:, width:]
            return carry

        steps = half // (group * rows)
        if steps > 8:
            lax.fori_loop(0, steps, go, 0)
        else:
            for g in range(steps):
                go(g, 0)

    step = 256

    def project(p):
        for l in range(own):
            both = wbuf.at[l, :, spans[p], :]
            pltpu.make_async_copy(both, both, gu_sem.at[l, p]).wait()
        for l in range(own):
            for n in range(0, hidden, step):
                cols = slice(n, min(n + step, hidden))
                gate, upper = (
                    jnp.dot(
                        x[:, spans[p]], wbuf[l, m, spans[p], cols],
                        preferred_element_type=jnp.float32,
                    )
                    for m in range(2)
                )
                if p > 0:
                    gate = gate + acc[l, 0, :, cols]
                    upper = upper + acc[l, 1, :, cols]
                if p < pieces - 1:
                    acc[l, 0, :, cols] = gate
                    acc[l, 1, :, cols] = upper
                else:
                    h[l, :, cols] = (gate / (1.0 + jnp.exp(-gate)) * upper).astype(jnp.bfloat16)

    for p in range(pieces):
        z_relay(p)
        if p == 0:
            gu_start(ahead, pieces)
            dn_start(0, 2)
        if p + 1 < pieces:
            pass_q(p + 1, z)
    q_relay(0, 0, nz)
    dn_start(2, nc)
    lay(0, e)
    for p in range(pieces):
        if p + 1 < pieces:
            q_relay(p + 1, 0, nz)
        await_e(p)
        lay(p, other)
        if p + 1 < pieces:
            lay(p + 1, e)
        project(p)

    lanes = lax.broadcasted_iota(jnp.int32, (tokens, LANES), 1)
    first = e * experts + r * own
    scales = [
        jnp.sum(jnp.where(lanes == first + l, wst[...], 0.0), axis=1, keepdims=True)
        for l in range(own)
    ]

    def ex_copy(c):
        return pltpu.make_async_remote_copy(
            src_ref=ex_send.at[c], dst_ref=ex_recv.at[c],
            send_sem=s_send.at[0], recv_sem=ex_rsem.at[c // 2],
            device_id={"exp": other}, device_id_type=MESH,
        )

    def sq_copies(c):
        if c < early:
            pairs = [
                (crossed((a + d) % nr, i), d * nr + i, crossed((a + d) % nr, b))
                for d in range(1, nr)
                for i in range(nr)
            ]
        else:
            pairs = [(moved(d), d, moved(d)) for d in range(1, nq)]
        return [
            pltpu.make_async_remote_copy(
                src_ref=q_send.at[c, block], dst_ref=q_recv.at[c, place],
                send_sem=s_send.at[1], recv_sem=q_rsem.at[c],
                device_id=device(target, z), device_id_type=MESH,
            )
            for block, place, target in pairs
        ]

    def f_copy(c, d):
        if c < early:
            place = (b * nz + z + d) % (nr * nz)
            target = device(crossed(a, place // nz), place % nz)
        else:
            place = near(nz - d)
            target = device(q, place)
            d = (place - z + nz) % nz
        return pltpu.make_async_remote_copy(
            src_ref=f_send.at[c, place], dst_ref=f_recv.at[c, d],
            send_sem=s_send.at[2], recv_sem=f_rsem.at[c],
            device_id=target, device_id_type=MESH,
        )

    def q_count(c):
        return (nr - 1) * nr if c < early else nq - 1

    def f_count(c):
        return nr * nz if c < early else nz

    def some(buffer, c, count, i, recv_sem):
        blocks = buffer.at[c, pl.ds(0, count)]
        return pltpu.make_async_remote_copy(
            src_ref=blocks, dst_ref=blocks, send_sem=s_send.at[i], recv_sem=recv_sem.at[c],
            device_id={"exp": other}, device_id_type=MESH,
        )

    def sum_drain(low, high):
        for c in range(low, high):
            ex_copy(c).wait_send()
            some(q_send, c, q_count(c), 1, q_rsem).wait_send()
            some(f_send, c, f_count(c) - 1, 2, f_rsem).wait_send()

    def down(chunks):
        for l in range(own):
            both = dbuf.at[l, pl.ds(chunks[0], len(chunks))]
            pltpu.make_async_copy(both, both, dn_sem.at[l, chunks[0] // 2]).wait()
        for c in chunks:
            for n in range(0, cw, step):
                cols = slice(n, min(n + step, cw))
                total = None
                for l in range(own):
                    value = scales[l] * jnp.dot(
                        h[l], dbuf[l, c, :, cols], preferred_element_type=jnp.float32
                    )
                    total = value if total is None else total + value
                low, high = total[:half], total[half:]
                keep[c, :, cols] = jnp.where(e == 0, low, high)
                ex_send[c, :, cols] = jnp.where(e == 0, high, low).astype(jnp.bfloat16)
        for c in chunks:
            ex_copy(c).start()

    def await_ex(chunks):
        blocks = ex_recv.at[pl.ds(chunks[0], len(chunks))]
        pltpu.make_async_remote_copy(
            src_ref=blocks, dst_ref=blocks, send_sem=s_send.at[0],
            recv_sem=ex_rsem.at[chunks[0] // 2], device_id={"exp": other}, device_id_type=MESH,
        ).wait_recv()

    def pass_ex(c):
        for qq in range(nq):
            span = slice(qq * part, (qq + 1) * part)
            total = keep[c, span, :] + ex_recv[c, span, :].astype(jnp.float32)
            q_send[c, qq] = total.astype(jnp.bfloat16)
            keep[c, span, :] = total
        for copy in sq_copies(c):
            copy.start()

    def kept(c, block):
        return keep[c, pl.ds(pl.multiple_of(block * part, part), part), :]

    def pass_q_sum(c):
        some(q_recv, c, q_count(c), 1, q_rsem).wait_recv()
        if c < early:
            sums = [
                sum(
                    (q_recv[c, d * nr + i].astype(jnp.float32) for d in range(1, nr)),
                    start=kept(c, crossed(a, i)),
                )
                for i in range(nr)
            ]
            mine = b * nz + z
        else:
            sums = [
                sum((q_recv[c, d].astype(jnp.float32) for d in range(1, nq)), start=kept(c, q))
            ]
            mine = z
        for i, total in enumerate(sums):
            for j in range(nz):
                f_send[c, i * nz + j] = total[j * rows:(j + 1) * rows, :].astype(jnp.bfloat16)
        f_recv[c, 0] = f_send[c, mine]
        for d in range(1, f_count(c)):
            f_copy(c, d).start()

    def collect(c):
        some(f_recv, c, f_count(c) - 1, 2, f_rsem).wait_recv()
        total = f_recv[c, 0].astype(jnp.float32)
        for d in range(1, f_count(c)):
            total += f_recv[c, d].astype(jnp.float32)
        out_ref[:, c * cw:(c + 1) * cw] = total.astype(out_ref.dtype)

    groups = [range(c, min(c + 2, nc)) for c in range(0, nc, 2)]
    for i, chunks in enumerate(groups):
        down(chunks)
        if i >= 2:
            await_ex(groups[i - 2])
            for c in groups[i - 2]:
                pass_ex(c)
    gather_drain()
    for chunks in groups[-2:]:
        await_ex(chunks)
        for c in chunks:
            pass_ex(c)
    for c in range(nc):
        pass_q_sum(c)
    for c in range(nc):
        if c == nc - 1:
            sum_drain(0, nc - 1)
        collect(c)
    sum_drain(nc - 1, nc)


def body(tokens, expert_ids, gate_ints, gate_weight, up_weight, down_weight):
    rows, width = tokens.shape
    experts, _, hidden = gate_weight.shape
    nt = lax.axis_size("tp")
    nr = lax.axis_size("rep")
    ny = 1
    while nt % (ny * 2) == 0 and (ny * 2) ** 2 <= nt:
        ny *= 2
    nz = nt // ny
    assert experts % nr == 0 and lax.axis_size("exp") == 2
    own = experts // nr
    slots = nt * nr * 2
    total = slots * rows
    cuts = (0, 1, 2, 4)
    pieces = len(cuts) - 1
    cw = min(256, width)
    nc = width // cw
    early = nc * 5 // 8 if nr == ny else 0
    ends = nt if early else nz
    bf16, f32, i32 = jnp.bfloat16, jnp.float32, jnp.int32
    vmem = pl.BlockSpec(memory_space=pltpu.VMEM)
    hbm = pl.BlockSpec(memory_space=pl.ANY)
    dma = pltpu.SemaphoreType.DMA
    nq = nr * ny
    part = total // 2 // nq
    top = expert_ids.shape[1]
    return pl.pallas_call(
        functools.partial(kernel, (nr, ny, nz, own), cw, cuts, early),
        out_shape=pltpu.VMEM((rows, width), bf16),
        in_specs=[hbm] * 6,
        out_specs=vmem,
        scratch_shapes=[
            pltpu.VMEM((top, rows), i32),
            pltpu.VMEM((top, rows), i32),
            pltpu.VMEM((slots, rows, width + LANES), bf16),
            pltpu.VMEM((16, width + LANES), f32),
            pltpu.VMEM((total, width), bf16),
            pltpu.VMEM((total, LANES), f32),
            pltpu.VMEM((own, 2, total, hidden), f32),
            pltpu.VMEM((own, total, hidden), bf16),
            pltpu.VMEM((own, 2, width, hidden), bf16),
            pltpu.VMEM((own, nc, hidden, cw), bf16),
            pltpu.VMEM((nc, total // 2, cw), f32),
            pltpu.VMEM((nc, total // 2, cw), bf16),
            pltpu.VMEM((nc, total // 2, cw), bf16),
            pltpu.VMEM((nc, nq, part, cw), bf16),
            pltpu.VMEM((nc, nq, part, cw), bf16),
            pltpu.VMEM((nc, ends, rows, cw), bf16),
            pltpu.VMEM((nc, ends, rows, cw), bf16),
            dma((2 + pieces,)),
            dma((own, pieces)),
            dma((own, -(-nc // 2))),
            dma((3,)),
            dma((pieces, nz)),
            dma((pieces, nz)),
            dma((pieces,)),
            dma((3,)),
            dma((-(-nc // 2),)),
            dma((nc,)),
            dma((nc,)),
        ],
        compiler_params=pltpu.CompilerParams(
            collective_id=0, has_side_effects=True, vmem_limit_bytes=VMEM_BYTES
        ),
    )(expert_ids.T, gate_ints.T, tokens, gate_weight, up_weight, down_weight)


def solution(mesh):
    return jax.shard_map(
        body,
        mesh=mesh,
        in_specs=(
            P(("rep", "exp", "tp"), None),
            P(("rep", "exp", "tp"), None),
            P(("rep", "exp", "tp"), None),
            P("exp", None, "tp"),
            P("exp", None, "tp"),
            P("exp", "tp", None),
        ),
        out_specs=P(("rep", "exp", "tp"), None),
        check_vma=False,
    )
```
